32 devices in a mesh: ctx: 8 (over y, x, core), chan: 4 (over z).
Axes of the slice: x: 2, y: 2, z: 4, core: 2. Of those that a mesh axis runs over, the one named last changes fastest.
Arguments:
- features: bfloat16 [3, 8192, 4096], P(None, 'chan', 'ctx'), may hold values from -6 to 6
- short_filter: float32 [3, 3, 8192], P(None, None, 'chan'), may hold values from -3.5 to 3.5
- lengths: int32 [8], P('ctx'), may hold values from 64 to 512, as said below
- offsets: int32 [8], P('ctx'), may hold values from 0 to 8128, as said below
- decay_rates: float32 [16, 1024], P(None, 'chan'), may hold values from 0 to 1, as said below
- residues: float32 [16, 1024], P(None, 'chan'), may hold values from -1 to 1
- skip_weight: float32 [8192], P('chan'), may hold values from -1 to 1
- out_weight: bfloat16 [8192, 4096], P('chan'), may hold values from -0.09375 to 0.09375
Outputs:
- projected: bfloat16 [4096, 4096], P('chan', 'ctx')
The draws below stay inside these ranges and needn't reach their ends.
Inputs may be any that keep to these rules, and one draw needn't show every extreme that they name: `lengths`: used slots of each shard, counted from slot 0; some shard uses all 512 slots and some only 64. offsets[i] + lengths[i] <= offsets[i + 1]; the first offset is 0. `decay_rates`: positive rates.
All inputs are finite; a program needn't handle non-finite values.
Results may differ from the reference program's by a relative error of at most 0.018.
Values may be sent and summed in bfloat16 or wider, within the bound.
No kernel may reach another device: no remote copies, remote signals or barrier semaphores. Data moves between devices by JAX's collectives and lax.ppermute only.
A program may use at most 192 MiB of HBM per device.

```python
import math
import jax
import jax.numpy as jnp
from jax import lax

D = 8192
GROUPS = 1024
MODES = 16
OUTW = 4096
KS = 3
LMAX = 512
TOKENS = 4096
N_CHAN = 4


def span_layout(key):
    shard_total = TOKENS // LMAX
    key_list = jax.random.split(jax.random.fold_in(key, 7), 5)
    drawn_lengths = jax.random.randint(key_list[0], (shard_total,), LMAX // 8, LMAX + 1)
    ranking = jax.random.permutation(key_list[1], shard_total)
    drawn_lengths = drawn_lengths.at[ranking[0]].set(LMAX).at[ranking[1]].set(LMAX // 8)
    spacing = jax.random.randint(key_list[2], (shard_total,), 0, LMAX // 8 + 1)
    chosen = jax.random.permutation(key_list[3], shard_total - 1)[:2] + 1
    wide_gaps = jax.random.randint(key_list[4], (2,), TOKENS // 4, TOKENS // 2 + 1)
    spacing = spacing.at[chosen].add(wide_gaps)
    preceding = jnp.concatenate([jnp.zeros((1,), jnp.int32), drawn_lengths[:-1]])
    starts = jnp.cumsum(spacing + preceding)
    starts = starts - starts[0]
    last_bound = (shard_total - 1) * (LMAX // 8 + LMAX) + TOKENS
    starts = starts.at[shard_total - 1].set(last_bound)
    return (drawn_lengths.astype(jnp.int32), starts.astype(jnp.int32))


def draw_lengths(key, part):
    return span_layout(key)[0]


def draw_offsets(key, part):
    return span_layout(key)[1]


def rate_table(key):
    key_list = jax.random.split(jax.random.fold_in(key, 13), 2)
    slow_share = 0.5
    chooser = jax.random.uniform(key_list[0], (MODES, GROUPS), jnp.float32)
    spread = jax.random.uniform(key_list[1], (MODES, GROUPS), jnp.float32)
    slow_rate = math.log(10.0) / (2.5 * TOKENS) * jnp.exp(math.log(0.4) * spread)
    fast_rate = 0.02 * jnp.exp(math.log(5.0) * spread)
    return jnp.where(chooser < slow_share, slow_rate, fast_rate)


def draw_decay_rates(key, part):
    return rate_table(key)


def draw_residues(key, part):
    table = rate_table(key)
    raw_values = jnp.clip(jax.random.normal(jax.random.fold_in(key, 17), (MODES, GROUPS), jnp.float32), -4.0, 4.0)
    return raw_values * jnp.sqrt(2.0 * table / MODES)


def raised(entries, own_key, source, target, shards_of, factor):
    owner, partner = [(jnp.arange(entries.shape[dim]) // (entries.shape[dim] // shards_of)).reshape([-1 if axis == dim else 1 for axis in range(entries.ndim)]) for dim in (source, target)]
    chosen = jax.random.permutation(own_key, shards_of)[partner]
    strong = (owner == chosen) | (owner == (partner + shards_of // 2) % shards_of)
    return jnp.where(strong, factor * entries, entries)


def block_levels(stream_key, shape, cuts, smallest, largest):
    def one(dim, shards_of):
        heights = jax.random.uniform(jax.random.fold_in(jax.random.fold_in(stream_key, 6), dim), (shards_of,), jnp.float32, smallest / len(cuts), largest / len(cuts))
        return jnp.repeat(jnp.exp(heights), shape[dim] // shards_of).reshape((-1,) + (1,) * (len(shape) - dim - 1))

    level = one(*cuts[0])
    for cut in cuts[1:]:
        level = level * one(*cut)
    return level


def normal_values(stream_key, extent, scale, limit, shards=(), held_as=jnp.bfloat16):
    level = block_levels(stream_key, extent, shards, -0.22, 0.18) if shards else 1.0
    drawn = jax.random.normal(stream_key, extent, jnp.float32) * scale * level
    return jnp.minimum(jnp.maximum(drawn, -limit), limit).astype(held_as)


def noise_with(rng, extent, scale, limit, cuts, heavy, held_as=jnp.bfloat16):
    result = scale * jax.random.normal(rng, extent, jnp.float32)
    if cuts:
        result = result * block_levels(rng, extent, cuts, -0.22, 0.18)
    return jnp.clip(raised(result, jax.random.fold_in(rng, 3), *heavy), -limit, limit).astype(held_as)


def setup_inputs(seed: int = 0) -> dict:
    splits = jax.random.split(jax.random.key(seed), 9)
    return {
        "features": normal_values(splits[0], (3, D, TOKENS), 1.0, 6.0, ((1, 4), (2, 8))),
        "short_filter": normal_values(splits[1], (3, KS, D), KS ** -0.5, 3.5, ((2, 4),), jnp.float32),
        "lengths": draw_lengths(jax.random.fold_in(splits[8], 71), 0),
        "offsets": draw_offsets(jax.random.fold_in(splits[8], 71), 0),
        "decay_rates": draw_decay_rates(jax.random.fold_in(splits[8], 71), 0),
        "residues": draw_residues(jax.random.fold_in(splits[8], 71), 0),
        "skip_weight": jnp.clip(jax.random.uniform(splits[6], (D,), jnp.float32, -1.0, 1.0) * block_levels(splits[6], (D,), ((0, 4),), -0.4, 0.0), -1.0, 1.0),
        "out_weight": noise_with(splits[7], (D, OUTW), D ** -0.5, 0.09375, ((0, 4),), (0, 1, 4, 2.0)),
    }


def reference(features, short_filter, lengths, offsets, decay_rates, residues, skip_weight, out_weight):
    per_group = D // GROUPS
    block_channels = D // N_CHAN
    slot_index = jnp.arange(TOKENS, dtype=jnp.int32)
    shard_index = slot_index // LMAX
    within = slot_index % LMAX
    usable = within < lengths[shard_index]
    position = (offsets[shard_index] + within).astype(jnp.float32)
    before = jnp.maximum(shard_index - 1, 0)
    sources = []
    present = []
    for tap_index in range(KS):
        source_slot = jnp.where(within >= tap_index, slot_index - tap_index, before * LMAX + lengths[before] + within - tap_index)
        sources.append(jnp.clip(source_slot, 0, TOKENS - 1).astype(jnp.int32))
        present.append((within >= tap_index) | (shard_index > 0))
    decay_chan = jnp.repeat(decay_rates, per_group, axis=1)
    residue_chan = jnp.repeat(residues, per_group, axis=1)

    def channel_block(running, block_number):
        first_channel = (block_number * block_channels).astype(jnp.int32)
        block_rows = lax.dynamic_slice_in_dim(features, first_channel, block_channels, axis=1).astype(jnp.float32)
        filters = lax.dynamic_slice_in_dim(short_filter, first_channel, block_channels, axis=2)
        short_conv = jnp.zeros((3, block_channels, TOKENS), jnp.float32)
        for tap_index in range(KS):
            taken_rows = jnp.take(block_rows, sources[tap_index], axis=2)
            short_conv = short_conv + filters[:, tap_index, :, None] * jnp.where(present[tap_index], taken_rows, 0.0)
        product = jnp.where(usable, short_conv[1] * short_conv[2], 0.0)
        rate_rows = lax.dynamic_slice_in_dim(decay_chan, first_channel, block_channels, axis=1)
        residue_rows = lax.dynamic_slice_in_dim(residue_chan, first_channel, block_channels, axis=1)

        def advance(carried, inputs):
            state_now, last_pos, started = carried
            column, here_pos, live_now = inputs
            gap_size = jnp.where(started > 0, here_pos - last_pos, 0.0)
            moved = jnp.exp(-rate_rows * gap_size) * state_now + column[None, :]
            state_now = jnp.where(live_now, moved, state_now)
            last_pos = jnp.where(live_now, here_pos, last_pos)
            started = jnp.maximum(started, live_now.astype(jnp.float32))
            return (state_now, last_pos, started), jnp.sum(residue_rows * state_now, axis=0)

        start_state = (jnp.zeros((MODES, block_channels), jnp.float32), jnp.zeros((), jnp.float32), jnp.zeros((), jnp.float32))
        ignored, conv_rows = lax.scan(advance, start_state, (product.T, position, usable))
        conv_rows = conv_rows.T
        skip_rows = lax.dynamic_slice_in_dim(skip_weight, first_channel, block_channels)
        mixed_rows = jnp.where(usable, short_conv[0] * (conv_rows + skip_rows[:, None] * product), 0.0).astype(jnp.bfloat16)
        weight_rows = lax.dynamic_slice_in_dim(out_weight, first_channel, block_channels, axis=0)
        partial_value = lax.dot_general(weight_rows, mixed_rows, (((0,), (0,)), ((), ())), preferred_element_type=jnp.float32)
        rounded = lax.optimization_barrier(partial_value.astype(jnp.bfloat16)).astype(jnp.float32)
        return running + rounded, None

    running, ignored = lax.scan(channel_block, jnp.zeros((OUTW, TOKENS), jnp.float32), jnp.arange(N_CHAN, dtype=jnp.int32))
    return running.astype(jnp.bfloat16)
```

```python
import functools

import jax
import jax.numpy as jnp
from jax import lax
from jax.experimental import pallas as pl
from jax.experimental.pallas import tpu as pltpu
from jax.sharding import PartitionSpec as P

F32 = jnp.float32
BF16 = jnp.bfloat16
W = 128
CB = 128
MB = 1 << 20


def dot(a, b, dims, precision=None):
    return lax.dot_general(a, b, (dims, ((), ())), precision=precision, preferred_element_type=F32)


def iota(shape, axis):
    return lax.broadcasted_iota(jnp.int32, shape, axis)


def call(body, out_shape, grid, in_specs, out_specs, prefetch=0, scratch=(), aliases=None, flops=0, nbytes=0, exps=0, name=None):
    return pl.pallas_call(
        body,
        out_shape=out_shape,
        grid_spec=pltpu.PrefetchScalarGridSpec(
            num_scalar_prefetch=prefetch, grid=grid, in_specs=in_specs, out_specs=out_specs, scratch_shapes=list(scratch)
        ),
        input_output_aliases=aliases or {},
        cost_estimate=pl.CostEstimate(flops=flops, bytes_accessed=nbytes, transcendentals=exps),
        compiler_params=pltpu.CompilerParams(vmem_limit_bytes=40 * MB),
        name=name,
    )


def rows_sum(x):
    return x[0] if len(x) == 1 else rows_sum(x[: len(x) // 2]) + rows_sum(x[len(x) // 2 :])


def tail_body(taps, info, near, far, out):
    length = info[0]
    acc = None
    for r in range(3):
        for k in range(taps - 1):
            slot = length - (taps - 1) + k
            src = near if k == taps - 2 else far
            pick = (iota((8, W), 0) == r * (taps - 1) + k) & (iota((8, W), 1) == lax.rem(slot, W))
            term = dot(pick.astype(BF16), src[r], ((1,), (1,)))
            acc = term if acc is None else acc + term
    out[...] = acc


def columns(par, halo):
    rows = par.shape[0] + halo.shape[0]
    full = jnp.concatenate([par, halo, jnp.zeros((CB - rows, CB), F32)], axis=0)
    return jnp.transpose(full)


def short_conv(x, cols, r, halo_at, lane):
    w0, w1, w2 = (cols[:, r * 3 + k : r * 3 + k + 1] for k in range(3))
    before2 = cols[:, halo_at + 2 * r : halo_at + 2 * r + 1]
    before1 = cols[:, halo_at + 2 * r + 1 : halo_at + 2 * r + 2]
    last1, last2 = before1, jnp.where(lane < 1, before2, before1)
    out = []
    for tile in x:
        roll1, roll2 = pltpu.roll(tile, 1, 1), pltpu.roll(tile, 2, 1)
        out.append(w0 * tile + w1 * jnp.where(lane < 1, last1, roll1) + w2 * jnp.where(lane < 2, last2, roll2))
        last1, last2 = roll1, roll2
    return out


def tiles_of(block, chunks):
    return [block[:, j * W : (j + 1) * W].astype(F32) for j in range(chunks)]


def group_rows(table, at, groups):
    shifted = pltpu.roll(table, lax.rem(W - at, W), 1)
    return [shifted[:, g : g + 1] for g in range(groups)], shifted


def product_body(chunks, blocks, info, k_ref, v_ref, halo, par, rates, p_ref, sq_ref, st_ref, rc_ref):
    i = pl.program_id(0)
    length, last_hi, last_lo = info[0], info[2], info[3]
    modes = rates.shape[0]

    @pl.when(i < blocks)
    def _():
        per = 8
        groups = CB // per
        lane = iota((CB, W), 1)
        cols = columns(par[...], halo[...])
        at = par.shape[0]
        key = short_conv(tiles_of(k_ref[0], chunks), cols, 1, at, lane)
        val = short_conv(tiles_of(v_ref[0], chunks), cols, 2, at, lane)
        prod = [jnp.where(lane + j * W < length, key[j] * val[j], 0.0).astype(BF16) for j in range(chunks)]
        for j in range(chunks):
            p_ref[:, j * W : (j + 1) * W] = prod[j]
        col, shifted = group_rows(rates[...], lax.rem(i * groups, W), groups)
        lag = iota((modes, W), 1)
        ahead = jnp.concatenate([jnp.exp(-c * (W - lag).astype(F32)) for c in col], axis=0).astype(BF16)
        last_chunk = lax.div(length - 1, W)
        left = length - 1 - last_chunk * W - lag
        reach = jnp.where(left >= 0, left, 0).astype(F32)
        ending = jnp.concatenate([jnp.where(left >= 0, jnp.exp(-c * reach), 0.0) for c in col], axis=0).astype(BF16)
        own = iota((groups * modes, CB), 0) // modes == iota((groups * modes, CB), 1) // per
        last = prod[0]
        for j in range(1, chunks):
            last = jnp.where(last_chunk == j, prod[j], last)

        def block_diagonal(table, tile):
            full = jnp.where(own, dot(table, tile, ((1,), (1,))), 0.0)
            return rows_sum([full[g * modes : (g + 1) * modes] for g in range(groups)])

        expand = (iota((W, CB), 0) == iota((W, CB), 1) // per).astype(F32)
        rate_ch = dot(shifted, expand, ((1,), (0,)), lax.Precision.HIGHEST)
        rc_ref[...] = rate_ch
        total = block_diagonal(ending, last)
        for j in range(chunks):
            summary = block_diagonal(ahead, prod[j])
            sq_ref[j] = summary
            if j < chunks - 1:
                rest = length - 1 - W * (j + 1)
                factor = jnp.exp(-rate_ch * jnp.maximum(rest, 0).astype(F32))
                total = total + jnp.where(j < last_chunk, factor * summary, 0.0)
        st_ref[...] = total.astype(BF16)

    @pl.when(i == blocks)
    def _():
        row = iota((modes, CB), 0)
        st_ref[...] = jnp.where(row == 0, last_hi, jnp.where(row == 1, last_lo, 0)).astype(F32).astype(BF16)


def inner_body(chunks, info, q_ref, p_ref, halo, par, rates, residues, ut_ref, qt_ref, sp_ref):
    i = pl.program_id(0)
    length = info[0]
    modes = rates.shape[0]
    per = 8
    groups = CB // per
    taps3 = 9
    lane = iota((CB, W), 1)
    cols = columns(par[...], halo[...])
    query = short_conv(tiles_of(q_ref[0], chunks), cols, 0, par.shape[0], lane)
    skip = cols[:, taps3 : taps3 + 1]
    prod = tiles_of(p_ref[...], chunks)
    lane0 = lax.rem(i * groups, W)
    rate_col, _ = group_rows(rates[...], lane0, groups)
    res_col, _ = group_rows(residues[...], lane0, groups)
    lag = iota((modes, W), 1).astype(F32)
    upper = iota((W, W), 1) >= iota((W, W), 0)
    spread, inner = [], [[] for _ in range(chunks)]
    for g in range(groups):
        decayed = res_col[g] * jnp.exp(-rate_col[g] * lag)
        spread.append(decayed)
        taps = jnp.broadcast_to(jnp.sum(decayed, axis=0, keepdims=True), (W, W))
        toeplitz = jnp.where(upper, pltpu.roll(taps, 0, 1, stride=1, stride_axis=0), 0.0).astype(BF16)
        stacked = jnp.concatenate([prod[j][g * per : (g + 1) * per] for j in range(chunks)], axis=0).astype(BF16)
        result = dot(stacked, toeplitz, ((1,), (0,)))
        for j in range(chunks):
            inner[j].append(result[j * per : (j + 1) * per])
    sp_ref[...] = jnp.transpose(jnp.concatenate(spread, axis=0)).astype(BF16)
    for j in range(chunks):
        used = lane + j * W < length
        q = jnp.where(used, query[j], 0.0)
        u = q * (jnp.concatenate(inner[j], axis=0) + skip * prod[j])
        ut_ref[j * W : (j + 1) * W, :] = jnp.transpose(u).astype(BF16)
        qt_ref[j * W : (j + 1) * W, :] = jnp.transpose(q).astype(BF16)


def enter_body(chunks, shifts, info, *refs):
    got, (rc, sq, e_ref) = refs[:shifts], refs[shifts:]
    first = info[1]
    channels = rc.shape[1]
    rate = rc[...]
    state = jnp.zeros(rate.shape, F32)
    for ref in got:
        mark = ref[0:2, channels : channels + 128].astype(F32)
        gap = first.astype(F32) - (mark[0:1, 0:1] * 256.0 + mark[1:2, 0:1])
        state = state + jnp.exp(-rate * gap) * ref[:, 0:channels].astype(F32)
    over = jnp.exp(-rate * float(W))
    for j in range(chunks):
        e_ref[j] = state.astype(BF16)
        if j < chunks - 1:
            state = over * state + sq[j]


def project_body(blocks, info, ut, qt, sp, e_ref, w_ref, m_ref, out):
    @pl.when(pl.program_id(0) == 0)
    def _():
        modes = e_ref.shape[1]
        per = 8
        groups = CB // per
        own = iota((groups * modes, CB), 0) // modes == iota((groups * modes, CB), 1) // per
        for b in range(blocks):
            at = slice(b * CB, (b + 1) * CB)
            state = e_ref[0, :, at].astype(F32)
            diagonal = jnp.where(own, jnp.concatenate([state] * groups, axis=0), 0.0).astype(BF16)
            wide = slice(b * groups * modes, (b + 1) * groups * modes)
            outer = dot(sp[:, wide], diagonal, ((1,), (0,)))
            m_ref[:, at] = (ut[:, at].astype(F32) + qt[:, at].astype(F32) * outer).astype(BF16)

    out[...] = dot(m_ref[...], w_ref[...], ((1,), (0,))).astype(BF16)


def project_rest_body(info, m_ref, w_ref, out):
    out[...] = dot(m_ref[...], w_ref[...], ((1,), (0,))).astype(BF16)


def finish_body(parts, fresh, info, *refs):
    first, later = refs[0], refs[1]
    rest = refs[2 : 2 + parts]
    out = refs[-1]
    acc = jnp.where(info[5] == 0, first[...].astype(F32), later[...].astype(F32))
    for ref in rest:
        acc = acc + ref[...].astype(F32)
    done = jnp.transpose(acc).astype(BF16)
    if fresh:
        out[...] = jnp.zeros(out.shape, BF16)
        out[:, 0:W] = done
    else:
        out[...] = done


def shards(chan_count, ctx_count, features, short_filter, lengths, offsets, decay_rates, residues, skip_weight, out_weight):
    taps = short_filter.shape[1]
    channels, slots = features.shape[1], features.shape[2]
    modes, groups = decay_rates.shape
    out_width = out_weight.shape[1]
    chunks = slots // W
    blocks = channels // CB
    per_block = groups // blocks
    length, offset = lengths[0], offsets[0]
    rank = lax.axis_index("chan")
    flip = (rank >= chan_count // 2).astype(jnp.int32)
    depth = jnp.minimum(rank, chan_count - 1 - rank).astype(jnp.int32)
    last = offset + length - 1
    info = jnp.stack([length, offset, last // 256, last % 256, flip, depth])
    par = jnp.concatenate(
        [short_filter.reshape(3 * taps, channels), skip_weight[None], jnp.zeros((6, channels), F32)], axis=0
    )

    tail_width = 512
    tail = call(
        functools.partial(tail_body, taps),
        jax.ShapeDtypeStruct((8, channels), F32),
        (channels // tail_width,),
        [
            pl.BlockSpec((3, tail_width, W), lambda i, s: (0, i, lax.div(s[0] - 1, W))),
            pl.BlockSpec((3, tail_width, W), lambda i, s: (0, i, lax.div(s[0] - 2, W))),
        ],
        pl.BlockSpec((8, tail_width), lambda i, s: (0, i)),
        prefetch=1,
        nbytes=6 * channels * W * 2,
        name="tail",
    )(info, features, features)
    halo = lax.ppermute(tail, "ctx", [(i, i + 1) for i in range(ctx_count - 1)])

    inside = lambda i: jnp.minimum(i, blocks - 1)
    window = lambda i: inside(i) * per_block // W
    prod, sums, ends, rate_ch = call(
        functools.partial(product_body, chunks, blocks),
        (
            jax.ShapeDtypeStruct((channels, slots), BF16),
            jax.ShapeDtypeStruct((chunks, modes, channels), F32),
            jax.ShapeDtypeStruct((modes, channels + CB), BF16),
            jax.ShapeDtypeStruct((modes, channels), F32),
        ),
        (blocks + 1,),
        [
            pl.BlockSpec((1, CB, slots), lambda i, s: (1, inside(i), 0)),
            pl.BlockSpec((1, CB, slots), lambda i, s: (2, inside(i), 0)),
            pl.BlockSpec((8, CB), lambda i, s: (0, inside(i))),
            pl.BlockSpec((16, CB), lambda i, s: (0, inside(i))),
            pl.BlockSpec((modes, W), lambda i, s: (0, window(i))),
        ],
        (
            pl.BlockSpec((CB, slots), lambda i, s: (inside(i), 0)),
            pl.BlockSpec((chunks, modes, CB), lambda i, s: (0, 0, inside(i))),
            pl.BlockSpec((modes, CB), lambda i, s: (0, i)),
            pl.BlockSpec((modes, CB), lambda i, s: (0, inside(i))),
        ),
        prefetch=1,
        flops=20 * channels * slots,
        nbytes=6 * channels * slots,
        exps=modes * groups * 2 * W,
        name="product",
    )(info, features, features, halo, par, decay_rates)

    got = [lax.ppermute(ends, "ctx", [(i, i + k) for i in range(ctx_count - k)]) for k in range(1, ctx_count)]

    ut, qt, spread = call(
        functools.partial(inner_body, chunks),
        (
            jax.ShapeDtypeStruct((slots, channels), BF16),
            jax.ShapeDtypeStruct((slots, channels), BF16),
            jax.ShapeDtypeStruct((W, groups * modes), BF16),
        ),
        (blocks,),
        [
            pl.BlockSpec((1, CB, slots), lambda i, s: (0, i, 0)),
            pl.BlockSpec((CB, slots), lambda i, s: (i, 0)),
            pl.BlockSpec((8, CB), lambda i, s: (0, i)),
            pl.BlockSpec((16, CB), lambda i, s: (0, i)),
            pl.BlockSpec((modes, W), lambda i, s: (0, i * per_block // W)),
            pl.BlockSpec((modes, W), lambda i, s: (0, i * per_block // W)),
        ],
        (
            pl.BlockSpec((slots, CB), lambda i, s: (0, i)),
            pl.BlockSpec((slots, CB), lambda i, s: (0, i)),
            pl.BlockSpec((W, per_block * modes), lambda i, s: (0, i)),
        ),
        prefetch=1,
        flops=2 * channels * slots * W,
        nbytes=8 * channels * slots,
        exps=modes * groups * W,
        name="inner",
    )(info, features, prod, halo, par, decay_rates, residues)

    whole = lambda shape: pl.BlockSpec(shape, lambda i, s: (0,) * len(shape))
    enter = call(
        functools.partial(enter_body, chunks, len(got)),
        jax.ShapeDtypeStruct((chunks, modes, channels), BF16),
        (1,),
        [whole((modes, channels + CB))] * len(got) + [whole((modes, channels)), whole((chunks, modes, channels))],
        whole((chunks, modes, channels)),
        prefetch=1,
        nbytes=8 * modes * channels * 2,
        exps=8 * modes * channels,
        name="enter",
    )(info, *got, rate_ch, sums)

    half = chan_count // 2
    block_width = out_width // chan_count
    tile = min(512, block_width)
    per_out = block_width // tile

    def column(block, sub, s):
        return jnp.where(s[4] == 0, block, chan_count - 1 - block) * per_out + sub

    def project(q, operands):
        ut, qt, spread, enter, weight = operands
        mixed, far = call(
            functools.partial(project_body, blocks),
            (
                jax.ShapeDtypeStruct((W, channels), BF16),
                jax.ShapeDtypeStruct((W, (chan_count - 1) * block_width), BF16),
            ),
            ((chan_count - 1) * per_out,),
            [
                pl.BlockSpec((W, channels), lambda i, s: (q, 0)),
                pl.BlockSpec((W, channels), lambda i, s: (q, 0)),
                pl.BlockSpec((W, groups * modes), lambda i, s: (0, 0)),
                pl.BlockSpec((1, modes, channels), lambda i, s: (q, 0, 0)),
                pl.BlockSpec((channels, tile), lambda i, s: (0, column(1 + i // per_out, i % per_out, s))),
            ],
            (
                pl.BlockSpec((W, channels), lambda i, s: (0, 0)),
                pl.BlockSpec((W, tile), lambda i, s: (0, i)),
            ),
            prefetch=1,
            flops=2 * W * channels * (chan_count - 1) * block_width,
            nbytes=2 * channels * (chan_count - 1) * block_width,
            name="project",
        )(info, ut, qt, spread, enter, weight)
        near = call(
            project_rest_body,
            jax.ShapeDtypeStruct((W, block_width), BF16),
            (per_out,),
            [
                pl.BlockSpec((W, channels), lambda i, s: (0, 0)),
                pl.BlockSpec((channels, tile), lambda i, s: (0, column(0, i, s))),
            ],
            pl.BlockSpec((W, tile), lambda i, s: (0, i)),
            prefetch=1,
            flops=2 * W * channels * block_width,
            nbytes=2 * channels * block_width,
            name="project_near",
        )(info, mixed, weight)
        return far, near

    def finish(q, buffer, far, near, parts):
        fresh = buffer is None
        specs = [
            pl.BlockSpec((W, block_width), lambda i, s: (0, 0)),
            pl.BlockSpec((W, block_width), lambda i, s: (0, jnp.maximum(s[5] - 1, 0))),
        ] + [pl.BlockSpec((W, block_width), lambda i, s: (0, 0))] * len(parts)
        arrays = [near, far, *parts]
        if not fresh:
            specs.append(pl.BlockSpec(memory_space=pl.ANY))
            arrays.append(buffer)
        return call(
            functools.partial(finish_body, len(parts), fresh),
            jax.ShapeDtypeStruct((block_width, slots), BF16),
            (1,),
            specs,
            pl.BlockSpec((block_width, slots if fresh else W), lambda i, s: (0, 0 if fresh else q)),
            prefetch=1,
            aliases=None if fresh else {len(arrays): 0},
            nbytes=(len(parts) + 2) * W * block_width * 2,
            name="finish",
        )(info, *arrays)

    def hop(step, array):
        return lax.ppermute(array, "chan", [(step - 1, step), (chan_count - step, chan_count - step - 1)])

    def reduce_line(far, near):
        parts = []
        for step in range(1, chan_count):
            if step <= half:
                mine = far[:, (step - 1) * block_width :]
            else:
                ends = chan_count - step
                pieces = [far[:, (b - 1) * block_width : b * block_width] for b in range(ends - 1, 0, -1)] + [near]
                mine = jnp.concatenate(pieces, axis=1) if len(pieces) > 1 else near
            if parts:
                mine = (mine.astype(F32) + parts[-1][:, block_width:].astype(F32)).astype(BF16)
            parts.append(hop(step, mine))
        return parts

    def branch(count):
        def run(operands):
            buffer = None
            for q in range(count):
                far, near = project(q, operands)
                parts = reduce_line(far, near)
                buffer = finish(q, buffer, far, near, parts)
            return buffer

        return run

    used = (length + (W - 1)) // W
    return lax.switch(used - 1, [branch(c + 1) for c in range(chunks)], (ut, qt, spread, enter, out_weight))


def solution(mesh):
    placed = (
        P(None, "chan", "ctx"),
        P(None, None, "chan"),
        P("ctx"),
        P("ctx"),
        P(None, "chan"),
        P(None, "chan"),
        P("chan"),
        P("chan", None),
    )
    body = functools.partial(shards, mesh.shape["chan"], mesh.shape["ctx"])
    return jax.shard_map(body, mesh=mesh, in_specs=placed, out_specs=P("chan", "ctx"), check_vma=False)
```

```python
import functools

import jax
import jax.numpy as jnp
from jax import lax
from jax.experimental import pallas as pl
from jax.experimental.pallas import tpu as pltpu
from jax.sharding import PartitionSpec as P

F32 = jnp.float32
BF16 = jnp.bfloat16
W = 128
CB = 128
MB = 1 << 20


def dot(a, b, dims, precision=None):
    return lax.dot_general(a, b, (dims, ((), ())), precision=precision, preferred_element_type=F32)


def iota(shape, axis):
    return lax.broadcasted_iota(jnp.int32, shape, axis)


def call(body, out_shape, grid, in_specs, out_specs, prefetch=0, scratch=(), aliases=None, flops=0, nbytes=0, exps=0, vmem=40, name=None):
    return pl.pallas_call(
        body,
        out_shape=out_shape,
        grid_spec=pltpu.PrefetchScalarGridSpec(
            num_scalar_prefetch=prefetch, grid=grid, in_specs=in_specs, out_specs=out_specs, scratch_shapes=list(scratch)
        ),
        input_output_aliases=aliases or {},
        cost_estimate=pl.CostEstimate(flops=flops, bytes_accessed=nbytes, transcendentals=exps),
        compiler_params=pltpu.CompilerParams(vmem_limit_bytes=vmem * MB),
        name=name,
    )


def rows_sum(x):
    return x[0] if len(x) == 1 else rows_sum(x[: len(x) // 2]) + rows_sum(x[len(x) // 2 :])


def tail_body(taps, info, near, far, out):
    length = info[0]
    acc = None
    for r in range(3):
        for k in range(taps - 1):
            slot = length - (taps - 1) + k
            src = near if k == taps - 2 else far
            pick = (iota((8, W), 0) == r * (taps - 1) + k) & (iota((8, W), 1) == lax.rem(slot, W))
            term = dot(pick.astype(BF16), src[r], ((1,), (1,)))
            acc = term if acc is None else acc + term
    out[...] = acc


def set_tables(shift, spots, sets):
    col = iota((2 * W, 2 * W), 1)
    source = jnp.where(col < W, col + (W - 1), col - 2)
    shift[...] = (iota((2 * W, 2 * W), 0) == source).astype(F32).astype(BF16)
    row, lane = iota((W, W), 0), iota((W, W), 1)
    for n, r in enumerate(sets):
        for k in range(3):
            pick = (row == 3 * r + k) | (row == 16 + 3 * r + k)
            spots[:, (4 * n + k) * W : (4 * n + k + 1) * W] = pick.astype(F32).astype(BF16)
        pick = (row == lane - (W - 2) + 32 + 2 * r) & (lane >= W - 2)
        spots[:, (4 * n + 3) * W : (4 * n + 4) * W] = pick.astype(F32).astype(BF16)
    if 4 * len(sets) * W < spots.shape[1]:
        pick = (row == 9) | (row == 25)
        spots[:, 4 * len(sets) * W :] = pick.astype(F32).astype(BF16)


def turned(x):
    eye = (iota((W, W), 0) == iota((W, W), 1)).astype(F32).astype(BF16)
    return dot(eye, x, ((1,), (1,)))


def columns(par, halo, spots):
    high = par.astype(BF16).astype(F32)
    full = jnp.concatenate([high, par - high, halo, jnp.zeros((CB - 40, CB), F32)], axis=0).astype(BF16)
    return dot(turned(full).astype(BF16), spots, ((1,), (0,)))


def short_conv(block, cols, n, shift, first, chunks):
    w0, w1, w2, before = (cols[:, (4 * n + k) * W : (4 * n + k + 1) * W] for k in range(4))
    tiles = [block[:, j * W : (j + 1) * W] if j >= 0 else before.astype(BF16) for j in range(first - 1, first + chunks)]
    pairs = jnp.concatenate([jnp.concatenate(tiles[j : j + 2], axis=1) for j in range(chunks)], axis=0)
    moved = dot(pairs, shift, ((1,), (0,)))
    out = []
    for j in range(chunks):
        rows = slice(j * CB, (j + 1) * CB)
        out.append(w0 * tiles[j + 1].astype(F32) + w1 * moved[rows, :W] + w2 * moved[rows, W:])
    return out


def tiles_of(block, chunks):
    return [block[:, j * W : (j + 1) * W].astype(F32) for j in range(chunks)]


def product_body(chunks, steps, sub, info, k_ref, v_ref, halo, par, rate_row, p_ref, sq_ref, st_ref, shift, spots):
    i = pl.program_id(0)
    length, last_hi, last_lo = info[0], info[2], info[3]
    modes = sq_ref.shape[1]
    per = 8
    wide = CB // per * modes

    @pl.when(i == 0)
    def _():
        set_tables(shift, spots, (1, 2))

    def block(b, carry):
        rows = pl.ds(pl.multiple_of(b * CB, CB), CB)
        lane = iota((CB, W), 1)
        cols = columns(par[:, rows], halo[:, rows], spots[...])
        key = short_conv(k_ref[0, rows, :], cols, 0, shift[...], 0, chunks)
        val = short_conv(v_ref[0, rows, :], cols, 1, shift[...], 0, chunks)
        prod = [jnp.where(lane + j * W < length, key[j] * val[j], 0.0).astype(BF16) for j in range(chunks)]
        for j in range(chunks):
            p_ref[rows, j * W : (j + 1) * W] = prod[j]
        rate = rate_row[:, pl.ds(pl.multiple_of(b * wide, wide), wide)]
        slot = iota((W, wide), 0)
        ahead = jnp.exp(-rate * (W - slot).astype(F32)).astype(BF16)
        last_chunk = lax.div(length - 1, W)
        left = length - 1 - last_chunk * W - slot
        ending = jnp.where(left >= 0, jnp.exp(-rate * jnp.maximum(left, 0).astype(F32)), 0.0).astype(BF16)
        own = iota((CB, wide), 0) // per == iota((CB, wide), 1) // modes
        last = prod[0]
        for j in range(1, chunks):
            last = jnp.where(last_chunk == j, prod[j], last)
        fold = (lax.rem(iota((modes, wide), 1), modes) == iota((modes, wide), 0)).astype(F32).astype(BF16)
        total = dot(last, ending, ((1,), (0,)))
        every = dot(jnp.concatenate(prod, axis=0), ahead, ((1,), (0,)))
        for j in range(chunks):
            summary = every[j * CB : (j + 1) * CB]
            if j < chunks - 1:
                sq_ref[j, :, rows] = dot(fold, jnp.where(own, summary, 0.0).astype(BF16), ((1,), (1,)))
                rest = jnp.maximum(length - 1 - W * (j + 1), 0).astype(F32)
                total = total + jnp.where(j < last_chunk, jnp.exp(-rate * rest), 0.0) * summary
        st_ref[:, rows] = dot(fold, jnp.where(own, total, 0.0).astype(BF16), ((1,), (1,))).astype(BF16)
        return carry

    @pl.when(i < steps)
    def _():
        lax.fori_loop(0, sub, block, 0, unroll=True)

    @pl.when(i == steps)
    def _():
        row = iota(st_ref.shape, 0)
        st_ref[...] = jnp.where(row == 0, last_hi, jnp.where(row == 1, last_lo, 0)).astype(F32).astype(BF16)


def inner_body(first, chunks, sub, info, q_ref, p_ref, halo, par, rates, rate_row, res_row, ut_ref, qt_ref, *rest):
    sp_ref, rc_ref = rest[:2] if first == 0 else (None, None)
    shift, spots = rest[-2:]
    i = pl.program_id(0)
    length = info[0]
    modes = rates.shape[0]
    per = 8
    groups = CB // per
    wide = groups * modes
    middle = W // 2

    @pl.when(i == 0)
    def _():
        set_tables(shift, spots, (0,))

    def block(b, carry):
        rows = pl.ds(pl.multiple_of(b * CB, CB), CB)
        lane = iota((CB, W), 1)
        cols = columns(par[:, rows], halo[:, rows], spots[...])
        query = short_conv(q_ref[0, rows, :], cols, 0, shift[...], first, chunks)
        skip = cols[:, 4 * W : 5 * W]
        prod = tiles_of(p_ref[rows, :], chunks)
        at = pl.ds(pl.multiple_of(b * wide, wide), wide)
        rate, res = rate_row[:, at], res_row[:, at]
        slot = iota((W, wide), 0).astype(F32)
        if first == 0:
            sp_ref[:, at] = (res * jnp.exp(-rate * slot)).astype(BF16)
        later = (res * jnp.exp(-rate * (slot - middle))).astype(BF16)
        sooner = jnp.exp(rate * (slot - middle)).astype(BF16)
        mine = iota((W, wide), 1) // modes
        upper = iota((W, W), 1) >= iota((W, W), 0)
        inner = [[] for _ in range(chunks)]
        kernels, stacks = [], []
        some = W // modes
        for h in range(groups // some):
            half = slice(h * W, h * W + W)
            left = jnp.concatenate(
                [jnp.where(mine[:, half] == h * some + g, sooner[:, half], jnp.zeros((W, W), BF16)) for g in range(some)], axis=0
            )
            full = dot(left, later[:, half], ((1,), (1,)))
            kernels += [jnp.where(upper, full[g * W : (g + 1) * W], 0.0).astype(BF16) for g in range(some)]
        for g in range(groups):
            stacks.append(jnp.concatenate([prod[j][g * per : (g + 1) * per] for j in range(chunks)], axis=0).astype(BF16))
        for g in range(groups):
            result = dot(stacks[g], kernels[g], ((1,), (0,)))
            for j in range(chunks):
                inner[j].append(result[j * per : (j + 1) * per])
        for j in range(chunks):
            used = lane + (first + j) * W < length
            q = jnp.where(used, query[j], 0.0)
            u = q * (jnp.concatenate(inner[j], axis=0) + skip * prod[j])
            ut_ref[j * W : (j + 1) * W, rows] = jnp.transpose(u.astype(BF16))
            qt_ref[j * W : (j + 1) * W, rows] = jnp.transpose(q.astype(BF16))
        if first > 0:
            return carry
        shifted = pltpu.roll(rates[...], lax.rem(W - lax.rem((i * sub + b) * groups, W), W), 1)
        expand = (iota((W, CB), 0) == iota((W, CB), 1) // per).astype(F32)
        rc_ref[:, rows] = dot(shifted, expand, ((1,), (0,)), lax.Precision.HIGHEST)
        return carry

    lax.fori_loop(0, sub, block, 0, unroll=2)


def enter_body(chunks, shifts, info, *refs):
    got, (rc, sq, e_ref) = refs[:shifts], refs[shifts:]
    first = info[1]
    channels = rc.shape[1]
    rate = rc[...]
    state = jnp.zeros(rate.shape, F32)
    for ref in got:
        mark = ref[0:2, channels : channels + 128].astype(F32)
        gap = first.astype(F32) - (mark[0:1, 0:1] * 256.0 + mark[1:2, 0:1])
        state = state + jnp.exp(-rate * gap) * ref[:, 0:channels].astype(F32)
    over = jnp.exp(-rate * float(W))
    for j in range(chunks):
        e_ref[j] = state.astype(BF16)
        if j < chunks - 1:
            state = over * state + sq[j]


def project_first_body(blocks, info, ut, qt, sp, e_ref, w_ref, m_ref, out):
    @pl.when(pl.program_id(0) == 0)
    def _():
        modes = e_ref.shape[1]
        per = 8
        groups = CB // per
        own = iota((groups * modes, CB), 0) // modes == iota((groups * modes, CB), 1) // per

        def block(b, carry):
            at = pl.ds(pl.multiple_of(b * CB, CB), CB)
            wide = pl.ds(pl.multiple_of(b * groups * modes, groups * modes), groups * modes)
            for c in range(e_ref.shape[0]):
                rows = slice(c * W, (c + 1) * W)
                state = e_ref[c, :, at].astype(F32)
                diagonal = jnp.where(own, jnp.concatenate([state] * groups, axis=0), 0.0).astype(BF16)
                outer = dot(sp[:, wide], diagonal, ((1,), (0,)))
                m_ref[rows, at] = (ut[rows, at].astype(F32) + qt[rows, at].astype(F32) * outer).astype(BF16)
            return carry

        lax.fori_loop(0, blocks, block, 0, unroll=2)

    out[...] = dot(m_ref[...], w_ref[...], ((1,), (0,))).astype(BF16)


def project_rest_body(per_out, info, m_ref, w_ref, *outs):
    i = pl.program_id(0)
    for k, out in enumerate(outs):

        @pl.when(i // per_out == k)
        def _(out=out):
            out[...] = dot(m_ref[...], w_ref[...], ((1,), (0,))).astype(BF16)


def finish_body(owns, fresh, rows, info, *refs):
    acc = refs[0][...].astype(F32)
    for k in range(1, owns):
        acc = jnp.where(info[5] == k, refs[k][...].astype(F32), acc)
    for ref in refs[owns : len(refs) - 1 - (not fresh)]:
        acc = acc + ref[...].astype(F32)
    out = refs[-1]
    done = jnp.transpose(acc).astype(BF16)
    if out.shape[1] > rows:
        out[:, :rows] = done
        out[:, rows:] = jnp.zeros((out.shape[0], out.shape[1] - rows), BF16)
    else:
        out[...] = done


def shards(chan_count, ctx_count, features, short_filter, lengths, offsets, decay_rates, residues, skip_weight, out_weight):
    taps = short_filter.shape[1]
    channels, slots = features.shape[1], features.shape[2]
    modes, groups = decay_rates.shape
    out_width = out_weight.shape[1]
    chunks = slots // W
    blocks = channels // CB
    per_block = groups // blocks
    length, offset = lengths[0], offsets[0]
    rank = lax.axis_index("chan")
    flip = (rank >= chan_count // 2).astype(jnp.int32)
    depth = jnp.minimum(rank, chan_count - 1 - rank).astype(jnp.int32)
    last = offset + length - 1
    info = jnp.stack([length, offset, last // 256, last % 256, flip, depth])
    par = jnp.concatenate(
        [short_filter.reshape(3 * taps, channels), skip_weight[None], jnp.zeros((6, channels), F32)], axis=0
    )

    tail_width = 512
    tail = call(
        functools.partial(tail_body, taps),
        jax.ShapeDtypeStruct((8, channels), F32),
        (channels // tail_width,),
        [
            pl.BlockSpec((3, tail_width, W), lambda i, s: (0, i, lax.div(s[0] - 1, W))),
            pl.BlockSpec((3, tail_width, W), lambda i, s: (0, i, lax.div(s[0] - 2, W))),
        ],
        pl.BlockSpec((8, tail_width), lambda i, s: (0, i)),
        prefetch=1,
        nbytes=6 * channels * W * 2,
        vmem=60,
        name="tail",
    )(info, features, features)
    halo = lax.ppermute(tail, "ctx", [(i, i + 1) for i in range(ctx_count - 1)])

    rows = jnp.transpose(jnp.stack([decay_rates, residues]), (0, 2, 1)).reshape(2, 1, groups * modes)
    rate_row, res_row = rows[0], rows[1]
    sub = 4
    step_channels = sub * CB
    steps = channels // step_channels
    inside = lambda i: jnp.minimum(i, steps - 1)
    tables = lambda sets, extra: [pltpu.VMEM((2 * W, 2 * W), BF16), pltpu.VMEM((W, (4 * sets + extra) * W), BF16)]
    prod, sums, ends = call(
        functools.partial(product_body, chunks, steps, sub),
        (
            jax.ShapeDtypeStruct((channels, slots), BF16),
            jax.ShapeDtypeStruct((chunks - 1, modes, channels), F32),
            jax.ShapeDtypeStruct((modes, channels + 128), BF16),
        ),
        (steps + 1,),
        [
            pl.BlockSpec((1, step_channels, slots), lambda i, s: (1, inside(i), 0)),
            pl.BlockSpec((1, step_channels, slots), lambda i, s: (2, inside(i), 0)),
            pl.BlockSpec((8, step_channels), lambda i, s: (0, inside(i))),
            pl.BlockSpec((16, step_channels), lambda i, s: (0, inside(i))),
            pl.BlockSpec((1, sub * per_block * modes), lambda i, s: (0, inside(i))),
        ],
        (
            pl.BlockSpec((step_channels, slots), lambda i, s: (inside(i), 0)),
            pl.BlockSpec((chunks - 1, modes, step_channels), lambda i, s: (0, 0, inside(i))),
            pl.BlockSpec((modes, step_channels), lambda i, s: (0, i)),
        ),
        prefetch=1,
        scratch=tables(2, 0),
        flops=20 * channels * slots,
        nbytes=6 * channels * slots,
        exps=modes * groups * 2 * W,
        vmem=60,
        name="product",
    )(info, features, features, halo, par, rate_row)
    got = [lax.ppermute(ends, "ctx", [(i, i + k) for i in range(ctx_count - k)]) for k in range(1, ctx_count)]

    def inner(first, count, info, prod):
        wide = sub * per_block * modes
        out_shape = [jax.ShapeDtypeStruct((count * W, channels), BF16)] * 2
        out_specs = [pl.BlockSpec((count * W, step_channels), lambda i, s: (0, i))] * 2
        if first == 0:
            out_shape += [jax.ShapeDtypeStruct((W, groups * modes), BF16), jax.ShapeDtypeStruct((modes, channels), F32)]
            out_specs += [pl.BlockSpec((W, wide), lambda i, s: (0, i)), pl.BlockSpec((modes, step_channels), lambda i, s: (0, i))]
        return call(
            functools.partial(inner_body, first, count, sub),
            out_shape,
            (steps,),
            [
                pl.BlockSpec((1, step_channels, slots), lambda i, s: (0, i, 0)),
                pl.BlockSpec((step_channels, count * W), lambda i, s: (i, first // count)),
                pl.BlockSpec((8, step_channels), lambda i, s: (0, i)),
                pl.BlockSpec((16, step_channels), lambda i, s: (0, i)),
                pl.BlockSpec((modes, W), lambda i, s: (0, i * sub * per_block // W)),
                pl.BlockSpec((1, wide), lambda i, s: (0, i)),
                pl.BlockSpec((1, wide), lambda i, s: (0, i)),
            ],
            out_specs,
            prefetch=1,
            scratch=tables(1, 1),
            flops=2 * channels * count * W * W,
            nbytes=8 * channels * count * W,
            exps=modes * groups * W,
            vmem=60,
            name="inner",
        )(info, features, prod, halo, par, decay_rates, rate_row, res_row)

    lead = min(2, chunks)
    ut, qt, spread, rate_ch = inner(0, chunks, info, prod)

    whole = lambda shape: pl.BlockSpec(shape, lambda i, s: (0,) * len(shape))
    enter = call(
        functools.partial(enter_body, chunks, len(got)),
        jax.ShapeDtypeStruct((chunks, modes, channels), BF16),
        (1,),
        [whole((modes, channels + CB))] * len(got) + [whole((modes, channels)), whole((chunks - 1, modes, channels))],
        whole((chunks, modes, channels)),
        prefetch=1,
        nbytes=8 * modes * channels * 2,
        exps=8 * modes * channels,
        name="enter",
    )(info, *got, rate_ch, sums)

    half = chan_count // 2
    block_width = out_width // chan_count
    tile = min(1024, block_width)
    per_out = block_width // tile

    def column(block, sub, s):
        return jnp.where(s[4] == 0, block, chan_count - 1 - block) * per_out + sub

    def project_first(first, count, info, operands):
        ut, qt, spread, enter, weight = operands
        return call(
            functools.partial(project_first_body, blocks),
            (jax.ShapeDtypeStruct((count * W, channels), BF16), jax.ShapeDtypeStruct((count * W, block_width), BF16)),
            (per_out,),
            [
                pl.BlockSpec((count * W, channels), lambda i, s: (first // count, 0)),
                pl.BlockSpec((count * W, channels), lambda i, s: (first // count, 0)),
                pl.BlockSpec((W, groups * modes), lambda i, s: (0, 0)),
                pl.BlockSpec((count, modes, channels), lambda i, s: (first // count, 0, 0)),
                pl.BlockSpec((channels, tile), lambda i, s: (0, column(chan_count - 1, i, s))),
            ],
            (
                pl.BlockSpec((count * W, channels), lambda i, s: (0, 0)),
                pl.BlockSpec((count * W, tile), lambda i, s: (0, i)),
            ),
            prefetch=1,
            flops=2 * count * W * channels * (block_width + modes * CB // 8),
            nbytes=2 * channels * (block_width + 4 * count * W),
            vmem=60,
            name="project_first",
        )(info, ut, qt, spread, enter, weight)

    def project_rest(count, info, mixed, weight):
        number = chan_count - 1
        return call(
            functools.partial(project_rest_body, per_out),
            [jax.ShapeDtypeStruct((count * W, block_width), BF16)] * number,
            (number * per_out,),
            [
                pl.BlockSpec((count * W, channels), lambda i, s: (0, 0)),
                pl.BlockSpec((channels, tile), lambda i, s: (0, column(number - 1 - i // per_out, lax.rem(i, per_out), s))),
            ],
            [
                pl.BlockSpec((count * W, tile), lambda i, s, k=k: (0, jnp.clip(i - k * per_out, 0, per_out - 1)))
                for k in range(number)
            ],
            prefetch=1,
            flops=2 * count * W * channels * number * block_width,
            nbytes=2 * channels * number * block_width,
            vmem=60,
            name="project_rest",
        )(info, mixed, weight)

    def finish(first, count, buffer, own, parts):
        fresh = buffer is None
        rows = count * W
        specs = [pl.BlockSpec((rows, block_width), lambda i, s: (0, 0))] * (len(own) + len(parts))
        arrays = [*own, *parts]
        if not fresh:
            specs = specs + [pl.BlockSpec(memory_space=pl.ANY)]
            arrays.append(buffer)
        return call(
            functools.partial(finish_body, len(own), fresh, rows),
            jax.ShapeDtypeStruct((block_width, slots), BF16),
            (1,),
            specs,
            pl.BlockSpec((block_width, slots if fresh else rows), lambda i, s: (0, 0 if fresh else first // count)),
            prefetch=1,
            aliases=None if fresh else {len(arrays): 0},
            nbytes=(len(parts) + 2) * rows * block_width * 2,
            name="finish",
        )(info, *arrays)

    def hop(step, array):
        return lax.ppermute(array, "chan", [(step - 1, step), (chan_count - step, chan_count - step - 1)])

    def tied(value, *after):
        return lax.optimization_barrier((value, *after))[0]

    def branch(count):
        pieces = [(first, min(lead, count - first)) for first in range(0, count, lead)]

        def run(operands):
            weight = operands[-1]
            held, buffer = info, None
            sums, got = [{} for _ in pieces], [{} for _ in pieces]

            def send(p, step, block):
                mine = sums[p][block]
                if step > 1:
                    mine = (mine.astype(F32) + got[p][step - 1, block].astype(F32)).astype(BF16)
                lands = chan_count - 1 - block if step == half else block
                got[p][step, lands] = hop(step, mine)
                return mine

            def sent(step):
                return range(chan_count - 1, step - 1, -1) if step <= half else range(chan_count - step - 1, -1, -1)

            last = chan_count - 1
            for p, (first, size) in enumerate(pieces):
                mixed, sums[p][last] = project_first(first, size, held, operands)
                send(p, 1, last)
                held = tied(held, sums[p][last])
                if p:
                    held = tied(held, *[send(p - 1, 2, block) for block in list(sent(2))[1:]])
                rest = project_rest(size, held, mixed, weight)
                for k, block in enumerate(range(last - 1, -1, -1)):
                    sums[p][block] = rest[k]
                for block in range(last - 1, 0, -1):
                    send(p, 1, block)
                held = tied(held, rest[-1])
                if p + 1 < len(pieces):
                    held = tied(held, send(p, 2, last))
            for p, (first, size) in enumerate(pieces):
                for step in range(2, chan_count):
                    for block in sent(step):
                        lands = chan_count - 1 - block if step == half else block
                        if (step, lands) not in got[p]:
                            send(p, step, block)
                own = [sums[p][k] for k in range(half)]
                mine = [got[p][step, step if step < half else chan_count - 1 - step] for step in range(1, chan_count)]
                buffer = finish(first, size, buffer, own, mine)
            return buffer

        return run

    used = (length + (W - 1)) // W
    return lax.switch(used - 1, [branch(c + 1) for c in range(chunks)], (ut, qt, spread, enter, out_weight))


def solution(mesh):
    placed = (
        P(None, "chan", "ctx"),
        P(None, None, "chan"),
        P("ctx"),
        P("ctx"),
        P(None, "chan"),
        P(None, "chan"),
        P("chan"),
        P("chan", None),
    )
    body = functools.partial(shards, mesh.shape["chan"], mesh.shape["ctx"])
    return jax.shard_map(body, mesh=mesh, in_specs=placed, out_specs=P("chan", "ctx"), check_vma=False)
```

```python
import functools

import jax
import jax.numpy as jnp
from jax import lax
from jax.experimental import pallas as pl
from jax.experimental.pallas import tpu as pltpu
from jax.sharding import PartitionSpec as P

F32 = jnp.float32
BF16 = jnp.bfloat16
W = 128
CB = 128
MB = 1 << 20


def dot(a, b, dims, precision=None):
    return lax.dot_general(a, b, (dims, ((), ())), precision=precision, preferred_element_type=F32)


def iota(shape, axis):
    return lax.broadcasted_iota(jnp.int32, shape, axis)


def call(body, out_shape, grid, in_specs, out_specs, prefetch=0, scratch=(), aliases=None, flops=0, nbytes=0, exps=0, vmem=40, name=None):
    return pl.pallas_call(
        body,
        out_shape=out_shape,
        grid_spec=pltpu.PrefetchScalarGridSpec(
            num_scalar_prefetch=prefetch, grid=grid, in_specs=in_specs, out_specs=out_specs, scratch_shapes=list(scratch)
        ),
        input_output_aliases=aliases or {},
        cost_estimate=pl.CostEstimate(flops=flops, bytes_accessed=nbytes, transcendentals=exps),
        compiler_params=pltpu.CompilerParams(vmem_limit_bytes=vmem * MB),
        name=name,
    )


def rows_sum(x):
    return x[0] if len(x) == 1 else rows_sum(x[: len(x) // 2]) + rows_sum(x[len(x) // 2 :])


def tail_body(taps, width, info, near, every, out, far, sem):
    length = info[0]
    crossing = lax.rem(length - 1, W) == 0
    row, lane = iota((8, W), 0), iota((8, W), 1)

    def picked(src, places):
        acc = None
        for r in range(3):
            pick = functools.reduce(
                lambda x, y: x | y, [(row == r * (taps - 1) + k) & (lane == lax.rem(length - (taps - 1) + k, W)) for k in places]
            )
            term = dot(pick.astype(F32).astype(BF16), src[r], ((1,), (1,)))
            acc = term if acc is None else acc + term
        return acc

    @pl.when(jnp.logical_not(crossing))
    def _():
        out[...] = picked(near, range(taps - 1))

    @pl.when(crossing)
    def _():
        rows = pl.ds(pl.multiple_of(pl.program_id(0) * width, width), width)
        lanes = pl.ds(pl.multiple_of(lax.div(length - 2, W) * W, W), W)
        copy = pltpu.make_async_copy(every.at[:, rows, lanes], far, sem)
        copy.start()
        copy.wait()
        out[...] = picked(near, [taps - 2]) + picked(far, [taps - 3])


def set_tables(shift, spots, sets):
    col = iota((2 * W, 2 * W), 1)
    source = jnp.where(col < W, col + (W - 1), col - 2)
    shift[...] = (iota((2 * W, 2 * W), 0) == source).astype(F32).astype(BF16)
    row, lane = iota((W, W), 0), iota((W, W), 1)
    for n, r in enumerate(sets):
        for k in range(3):
            pick = (row == 3 * r + k) | (row == 16 + 3 * r + k)
            spots[:, (4 * n + k) * W : (4 * n + k + 1) * W] = pick.astype(F32).astype(BF16)
        pick = (row == lane - (W - 2) + 32 + 2 * r) & (lane >= W - 2)
        spots[:, (4 * n + 3) * W : (4 * n + 4) * W] = pick.astype(F32).astype(BF16)
    if 4 * len(sets) * W < spots.shape[1]:
        pick = (row == 9) | (row == 25)
        spots[:, 4 * len(sets) * W :] = pick.astype(F32).astype(BF16)


def turned(x):
    eye = (iota((W, W), 0) == iota((W, W), 1)).astype(F32).astype(BF16)
    return dot(eye, x, ((1,), (1,)))


def columns(par, halo, spots):
    high = par.astype(BF16).astype(F32)
    full = jnp.concatenate([high, par - high, halo, jnp.zeros((CB - 40, CB), F32)], axis=0).astype(BF16)
    return dot(turned(full).astype(BF16), spots, ((1,), (0,)))


def short_conv(block, cols, n, shift, first, chunks):
    w0, w1, w2, before = (cols[:, (4 * n + k) * W : (4 * n + k + 1) * W] for k in range(4))
    tiles = [block[:, j * W : (j + 1) * W] if j >= 0 else before.astype(BF16) for j in range(first - 1, first + chunks)]
    pairs = jnp.concatenate([jnp.concatenate(tiles[j : j + 2], axis=1) for j in range(chunks)], axis=0)
    moved = dot(pairs, shift, ((1,), (0,)))
    out = []
    for j in range(chunks):
        rows = slice(j * CB, (j + 1) * CB)
        out.append(w0 * tiles[j + 1].astype(F32) + w1 * moved[rows, :W] + w2 * moved[rows, W:])
    return out


def tiles_of(block, chunks):
    return [block[:, j * W : (j + 1) * W].astype(F32) for j in range(chunks)]


def product_body(chunks, steps, sub, info, k_ref, v_ref, halo, par, rate_row, p_ref, sq_ref, st_ref, shift, spots):
    i = pl.program_id(0)
    length, last_hi, last_lo = info[0], info[2], info[3]
    modes = sq_ref.shape[1]
    per = 8
    wide = CB // per * modes

    @pl.when(i == 0)
    def _():
        set_tables(shift, spots, (1, 2))

    def block(b, carry):
        rows = pl.ds(pl.multiple_of(b * CB, CB), CB)
        lane = iota((CB, W), 1)
        cols = columns(par[:, rows], halo[:, rows], spots[...])
        key = short_conv(k_ref[0, rows, :], cols, 0, shift[...], 0, chunks)
        val = short_conv(v_ref[0, rows, :], cols, 1, shift[...], 0, chunks)
        prod = [jnp.where(lane + j * W < length, key[j] * val[j], 0.0).astype(BF16) for j in range(chunks)]
        for j in range(chunks):
            p_ref[rows, j * W : (j + 1) * W] = prod[j]
        rate = rate_row[:, pl.ds(pl.multiple_of(b * wide, wide), wide)]
        slot = iota((W, wide), 0)
        ahead = jnp.exp(-rate * (W - slot).astype(F32)).astype(BF16)
        last_chunk = lax.div(length - 1, W)
        left = length - 1 - last_chunk * W - slot
        ending = jnp.where(left >= 0, jnp.exp(-rate * jnp.maximum(left, 0).astype(F32)), 0.0).astype(BF16)
        own = iota((CB, wide), 0) // per == iota((CB, wide), 1) // modes
        last = prod[0]
        for j in range(1, chunks):
            last = jnp.where(last_chunk == j, prod[j], last)
        fold = (lax.rem(iota((modes, wide), 1), modes) == iota((modes, wide), 0)).astype(F32).astype(BF16)
        total = dot(last, ending, ((1,), (0,)))
        every = dot(jnp.concatenate(prod, axis=0), ahead, ((1,), (0,)))
        for j in range(chunks):
            summary = every[j * CB : (j + 1) * CB]
            if j < chunks - 1:
                sq_ref[j, :, rows] = dot(fold, jnp.where(own, summary, 0.0).astype(BF16), ((1,), (1,)))
                rest = jnp.maximum(length - 1 - W * (j + 1), 0).astype(F32)
                total = total + jnp.where(j < last_chunk, jnp.exp(-rate * rest), 0.0) * summary
        st_ref[:, rows] = dot(fold, jnp.where(own, total, 0.0).astype(BF16), ((1,), (1,))).astype(BF16)
        return carry

    @pl.when(i < steps)
    def _():
        lax.fori_loop(0, sub, block, 0, unroll=True)

    @pl.when(i == steps)
    def _():
        row = iota(st_ref.shape, 0)
        st_ref[...] = jnp.where(row == 0, last_hi, jnp.where(row == 1, last_lo, 0)).astype(F32).astype(BF16)


def rates_body(info, rates, rc_ref):
    groups, channels = rates.shape[1], rc_ref.shape[1]
    expand = (iota((groups, channels), 0) == iota((groups, channels), 1) // (channels // groups)).astype(F32)
    rc_ref[...] = dot(rates[...], expand, ((1,), (0,)), lax.Precision.HIGHEST)


def inner_body(chunks, sub, modes, info, q_ref, p_ref, halo, par, rate_row, res_row, *rest):
    ut_ref, qt_ref, sp_ref, shift, spots = rest[-5:]
    i = pl.program_id(0)
    length = info[0]
    per = 8
    groups = CB // per
    wide = groups * modes
    middle = W // 2

    @pl.when(i == 0)
    def _():
        set_tables(shift, spots, (0,))

    def block(b, carry):
        rows = pl.ds(pl.multiple_of(b * CB, CB), CB)
        lane = iota((CB, W), 1)
        cols = columns(par[:, rows], halo[:, rows], spots[...])
        query = short_conv(q_ref[0, rows, :], cols, 0, shift[...], 0, chunks)
        skip = cols[:, 4 * W : 5 * W]
        prod = tiles_of(p_ref[rows, :], chunks)
        at = pl.ds(pl.multiple_of(b * wide, wide), wide)
        rate, res = rate_row[:, at], res_row[:, at]
        slot = iota((W, wide), 0).astype(F32)
        sp_ref[:, at] = (res * jnp.exp(-rate * slot)).astype(BF16)
        later = (res * jnp.exp(-rate * (slot - middle))).astype(BF16)
        sooner = jnp.exp(rate * (slot - middle)).astype(BF16)
        mine = iota((W, wide), 1) // modes
        upper = iota((W, W), 1) >= iota((W, W), 0)
        inner = [[] for _ in range(chunks)]
        kernels, stacks = [], []
        some = W // modes
        for h in range(groups // some):
            half = slice(h * W, h * W + W)
            left = jnp.concatenate(
                [jnp.where(mine[:, half] == h * some + g, sooner[:, half], jnp.zeros((W, W), BF16)) for g in range(some)], axis=0
            )
            full = dot(left, later[:, half], ((1,), (1,)))
            kernels += [jnp.where(upper, full[g * W : (g + 1) * W], 0.0).astype(BF16) for g in range(some)]
        for g in range(groups):
            stacks.append(jnp.concatenate([prod[j][g * per : (g + 1) * per] for j in range(chunks)], axis=0).astype(BF16))
        for g in range(groups):
            result = dot(stacks[g], kernels[g], ((1,), (0,)))
            for j in range(chunks):
                inner[j].append(result[j * per : (j + 1) * per])
        for j in range(chunks):
            used = lane + j * W < length
            q = jnp.where(used, query[j], 0.0)
            u = q * (jnp.concatenate(inner[j], axis=0) + skip * prod[j])
            ut_ref[j * W : (j + 1) * W, rows] = jnp.transpose(u.astype(BF16))
            qt_ref[j * W : (j + 1) * W, rows] = jnp.transpose(q.astype(BF16))
        return carry

    lax.fori_loop(0, sub, block, 0, unroll=2)


def position(ref, channels):
    mark = ref[0:2, channels : channels + 128].astype(F32)
    return mark[0:1, 0:1] * 256.0 + mark[1:2, 0:1]


def chip_body(info, own, other, rc, out):
    channels = rc.shape[1]
    rate = rc[...]
    here, there = position(own, channels), position(other, channels)
    last = jnp.maximum(here, there)
    state = jnp.exp(-rate * (last - here)) * own[:, 0:channels].astype(F32)
    state = state + jnp.exp(-rate * (last - there)) * other[:, 0:channels].astype(F32)
    out[:, 0:channels] = state.astype(BF16)
    mark, mark2 = own[:, channels : channels + 128], other[:, channels : channels + 128]
    out[:, channels : channels + 128] = jnp.where(there > here, mark2.astype(F32), mark.astype(F32)).astype(BF16)


def enter_body(chunks, shifts, info, *refs):
    got, (other, rc, sq, e_ref) = refs[:shifts], refs[shifts:]
    first = info[1].astype(F32)
    channels = rc.shape[1]
    rate = rc[...]
    gap = jnp.maximum(first - position(other, channels), 0.0)
    state = jnp.where(info[6] == 1, jnp.exp(-rate * gap) * other[:, 0:channels].astype(F32), 0.0)
    for ref in got:
        state = state + jnp.exp(-rate * (first - position(ref, channels))) * ref[:, 0:channels].astype(F32)
    over = jnp.exp(-rate * float(W))
    for j in range(chunks):
        e_ref[j] = state.astype(BF16)
        if j < chunks - 1:
            state = over * state + sq[j]


def project_first_body(sub, info, ut, qt, sp, e_ref, w_ref, m_ref, out, acc):
    k = pl.program_id(0)
    count, modes = e_ref.shape[:2]
    per = 8
    groups = CB // per
    own = iota((groups * modes, CB), 0) // modes == iota((groups * modes, CB), 1) // per
    for b in range(sub):
        at = slice(b * CB, (b + 1) * CB)
        diagonal = [
            jnp.where(own, jnp.concatenate([e_ref[c, :, at].astype(F32)] * groups, axis=0), 0.0).astype(BF16)
            for c in range(count)
        ]
        spread = sp[:, b * groups * modes : (b + 1) * groups * modes]
        outer = dot(spread, jnp.concatenate(diagonal, axis=1), ((1,), (0,)))
        for c in range(count):
            rows = slice(c * W, (c + 1) * W)
            gate = qt[rows, at].astype(F32) * outer[:, c * CB : (c + 1) * CB]
            m_ref[rows, at] = (ut[rows, at].astype(F32) + gate).astype(BF16)
    term = dot(m_ref[...], w_ref[...], ((1,), (0,)))

    @pl.when(k == 0)
    def _():
        acc[...] = term

    @pl.when(k > 0)
    def _():
        acc[...] += term

    @pl.when(k == pl.num_programs(0) - 1)
    def _():
        out[...] = acc[...].astype(BF16)


def project_rest_body(per_out, info, m_ref, w_ref, *outs):
    i = pl.program_id(0)
    for k, out in enumerate(outs):

        @pl.when(i // per_out == k)
        def _(out=out):
            out[...] = dot(m_ref[...], w_ref[...], ((1,), (0,))).astype(BF16)


def finish_body(owns, fresh, rows, info, *refs):
    acc = refs[0][...].astype(F32)
    for k in range(1, owns):
        acc = jnp.where(info[5] == k, refs[k][...].astype(F32), acc)
    for ref in refs[owns : len(refs) - 1 - (not fresh)]:
        acc = acc + ref[...].astype(F32)
    out = refs[-1]
    done = jnp.transpose(acc).astype(BF16)
    if out.shape[1] > rows:
        out[:, :rows] = done
        out[:, rows:] = jnp.zeros((out.shape[0], out.shape[1] - rows), BF16)
    else:
        out[...] = done


def shards(chan_count, ctx_count, features, short_filter, lengths, offsets, decay_rates, residues, skip_weight, out_weight):
    taps = short_filter.shape[1]
    channels, slots = features.shape[1], features.shape[2]
    modes, groups = decay_rates.shape
    out_width = out_weight.shape[1]
    chunks = slots // W
    blocks = channels // CB
    per_block = groups // blocks
    length, offset = lengths[0], offsets[0]
    rank = lax.axis_index("chan")
    flip = (rank >= chan_count // 2).astype(jnp.int32)
    depth = jnp.minimum(rank, chan_count - 1 - rank).astype(jnp.int32)
    last = offset + length - 1
    odd = lax.axis_index("ctx") % 2
    info = jnp.stack([length, offset, last // 256, last % 256, flip, depth, odd.astype(jnp.int32)])
    par = jnp.concatenate(
        [short_filter.reshape(3 * taps, channels), skip_weight[None], jnp.zeros((6, channels), F32)], axis=0
    )

    tail_width = 1024
    tail = call(
        functools.partial(tail_body, taps, tail_width),
        jax.ShapeDtypeStruct((8, channels), F32),
        (channels // tail_width,),
        [
            pl.BlockSpec((3, tail_width, W), lambda i, s: (0, i, lax.div(s[0] - 1, W))),
            pl.BlockSpec(memory_space=pl.ANY),
        ],
        pl.BlockSpec((8, tail_width), lambda i, s: (0, i)),
        prefetch=1,
        scratch=[pltpu.VMEM((3, tail_width, W), BF16), pltpu.SemaphoreType.DMA],
        nbytes=6 * channels * W,
        vmem=60,
        name="tail",
    )(info, features, features)
    halo = lax.ppermute(tail, "ctx", [(i, i + 1) for i in range(ctx_count - 1)])

    rows = jnp.transpose(jnp.stack([decay_rates, residues]), (0, 2, 1)).reshape(2, 1, groups * modes)
    rate_row, res_row = rows[0], rows[1]
    sub = 4
    step_channels = sub * CB
    steps = channels // step_channels
    inside = lambda i: jnp.minimum(i, steps - 1)
    tables = lambda sets, extra: [pltpu.VMEM((2 * W, 2 * W), BF16), pltpu.VMEM((W, (4 * sets + extra) * W), BF16)]
    whole = lambda shape: pl.BlockSpec(shape, lambda i, s: (0,) * len(shape))
    rate_ch = call(
        rates_body,
        jax.ShapeDtypeStruct((modes, channels), F32),
        (1,),
        [whole((modes, groups))],
        whole((modes, channels)),
        prefetch=1,
        nbytes=4 * modes * channels,
        vmem=60,
        name="rates",
    )(info, decay_rates)
    halo, _ = lax.optimization_barrier((halo, rate_ch))
    prod, sums, ends = call(
        functools.partial(product_body, chunks, steps, sub),
        (
            jax.ShapeDtypeStruct((channels, slots), BF16),
            jax.ShapeDtypeStruct((chunks - 1, modes, channels), F32),
            jax.ShapeDtypeStruct((modes, channels + 128), BF16),
        ),
        (steps + 1,),
        [
            pl.BlockSpec((1, step_channels, slots), lambda i, s: (1, inside(i), 0)),
            pl.BlockSpec((1, step_channels, slots), lambda i, s: (2, inside(i), 0)),
            pl.BlockSpec((8, step_channels), lambda i, s: (0, inside(i))),
            pl.BlockSpec((16, step_channels), lambda i, s: (0, inside(i))),
            pl.BlockSpec((1, sub * per_block * modes), lambda i, s: (0, inside(i))),
        ],
        (
            pl.BlockSpec((step_channels, slots), lambda i, s: (inside(i), 0)),
            pl.BlockSpec((chunks - 1, modes, step_channels), lambda i, s: (0, 0, inside(i))),
            pl.BlockSpec((modes, step_channels), lambda i, s: (0, i)),
        ),
        prefetch=1,
        scratch=tables(2, 0),
        flops=20 * channels * slots,
        nbytes=6 * channels * slots,
        exps=modes * groups * 2 * W,
        vmem=60,
        name="product",
    )(info, features, features, halo, par, rate_row)
    other = lax.ppermute(ends, "ctx", [(i, i ^ 1) for i in range(ctx_count)])
    wide = sub * per_block * modes
    cut = max(steps // 2, 1)

    def inner(first, count, info, before):
        at = lambda i: i + first
        return call(
            functools.partial(inner_body, chunks, sub, modes),
            (
                jax.ShapeDtypeStruct((slots, channels), BF16),
                jax.ShapeDtypeStruct((slots, channels), BF16),
                jax.ShapeDtypeStruct((W, groups * modes), BF16),
            ),
            (count,),
            [
                pl.BlockSpec((1, step_channels, slots), lambda i, s: (0, at(i), 0)),
                pl.BlockSpec((step_channels, slots), lambda i, s: (at(i), 0)),
                pl.BlockSpec((8, step_channels), lambda i, s: (0, at(i))),
                pl.BlockSpec((16, step_channels), lambda i, s: (0, at(i))),
                pl.BlockSpec((1, wide), lambda i, s: (0, at(i))),
                pl.BlockSpec((1, wide), lambda i, s: (0, at(i))),
            ]
            + [pl.BlockSpec(memory_space=pl.ANY)] * len(before),
            (
                pl.BlockSpec((slots, step_channels), lambda i, s: (0, at(i))),
                pl.BlockSpec((slots, step_channels), lambda i, s: (0, at(i))),
                pl.BlockSpec((W, wide), lambda i, s: (0, at(i))),
            ),
            prefetch=1,
            scratch=tables(1, 1),
            aliases={7 + k: k for k in range(len(before))},
            flops=2 * count * step_channels * slots * W,
            nbytes=8 * count * step_channels * slots,
            exps=3 * modes * groups * W * count // steps,
            vmem=60,
            name="inner",
        )(info, features, prod, halo, par, rate_row, res_row, *before)

    turned_first = inner(0, cut, info, ())
    other = lax.optimization_barrier((other, turned_first[2]))[0]
    chip = call(
        chip_body,
        jax.ShapeDtypeStruct(ends.shape, BF16),
        (1,),
        [whole(ends.shape)] * 2 + [whole((modes, channels))],
        whole(ends.shape),
        prefetch=1,
        nbytes=12 * modes * channels,
        exps=2 * modes * channels,
        vmem=60,
        name="chip",
    )(info, ends, other, rate_ch)
    got = [lax.ppermute(chip, "ctx", [(i, i + k) for i in range(ctx_count - k)]) for k in range(2, ctx_count, 2)]

    held = lax.optimization_barrier((info, chip))[0]
    ut, qt, spread = inner(cut, steps - cut, held, turned_first) if steps > cut else turned_first

    lead = min(2, chunks)
    enter = call(
        functools.partial(enter_body, chunks, len(got)),
        jax.ShapeDtypeStruct((chunks, modes, channels), BF16),
        (1,),
        [whole(ends.shape)] * (len(got) + 1) + [whole((modes, channels)), whole((chunks - 1, modes, channels))],
        whole((chunks, modes, channels)),
        prefetch=1,
        nbytes=8 * modes * channels * 2,
        exps=8 * modes * channels,
        vmem=60,
        name="enter",
    )(info, *got, other, rate_ch, sums)

    half = chan_count // 2
    block_width = out_width // chan_count
    tile = min(1024, block_width)
    per_out = block_width // tile

    def column(block, sub, s):
        return jnp.where(s[4] == 0, block, chan_count - 1 - block) * per_out + sub

    def project_first(first, count, info, operands):
        ut, qt, spread, enter, weight = operands
        return call(
            functools.partial(project_first_body, sub),
            (jax.ShapeDtypeStruct((count * W, channels), BF16), jax.ShapeDtypeStruct((count * W, block_width), BF16)),
            (steps,),
            [
                pl.BlockSpec((count * W, step_channels), lambda i, s: (first // count, i)),
                pl.BlockSpec((count * W, step_channels), lambda i, s: (first // count, i)),
                pl.BlockSpec((W, wide), lambda i, s: (0, i)),
                pl.BlockSpec((count, modes, step_channels), lambda i, s: (first // count, 0, i)),
                pl.BlockSpec((step_channels, block_width), lambda i, s: (i, jnp.where(s[4] == 0, chan_count - 1, 0))),
            ],
            (
                pl.BlockSpec((count * W, step_channels), lambda i, s: (0, i)),
                pl.BlockSpec((count * W, block_width), lambda i, s: (0, 0)),
            ),
            prefetch=1,
            scratch=[pltpu.VMEM((count * W, block_width), F32)],
            flops=2 * count * W * channels * (block_width + modes * CB // 8),
            nbytes=2 * channels * (block_width + 4 * count * W),
            vmem=60,
            name="project_first",
        )(info, ut, qt, spread, enter, weight)

    def project_rest(count, info, mixed, weight):
        number = chan_count - 1
        return call(
            functools.partial(project_rest_body, per_out),
            [jax.ShapeDtypeStruct((count * W, block_width), BF16)] * number,
            (number * per_out,),
            [
                pl.BlockSpec((count * W, channels), lambda i, s: (0, 0)),
                pl.BlockSpec((channels, tile), lambda i, s: (0, column(number - 1 - i // per_out, lax.rem(i, per_out), s))),
            ],
            [
                pl.BlockSpec((count * W, tile), lambda i, s, k=k: (0, jnp.clip(i - k * per_out, 0, per_out - 1)))
                for k in range(number)
            ],
            prefetch=1,
            flops=2 * count * W * channels * number * block_width,
            nbytes=2 * channels * number * block_width,
            vmem=60,
            name="project_rest",
        )(info, mixed, weight)

    def finish(first, count, buffer, own, parts):
        fresh = buffer is None
        rows = count * W
        specs = [pl.BlockSpec((rows, block_width), lambda i, s: (0, 0))] * (len(own) + len(parts))
        arrays = [*own, *parts]
        if not fresh:
            specs = specs + [pl.BlockSpec(memory_space=pl.ANY)]
            arrays.append(buffer)
        return call(
            functools.partial(finish_body, len(own), fresh, rows),
            jax.ShapeDtypeStruct((block_width, slots), BF16),
            (1,),
            specs,
            pl.BlockSpec((block_width, slots if fresh else rows), lambda i, s: (0, 0 if fresh else first // count)),
            prefetch=1,
            aliases=None if fresh else {len(arrays): 0},
            nbytes=(len(parts) + 2) * rows * block_width * 2,
            name="finish",
        )(info, *arrays)

    def hop(step, array):
        return lax.ppermute(array, "chan", [(step - 1, step), (chan_count - step, chan_count - step - 1)])

    def tied(value, *after):
        return lax.optimization_barrier((value, *after))[0]

    def branch(count):
        pieces = [(first, min(lead, count - first)) for first in range(0, count, lead)]

        def run(operands):
            weight = operands[-1]
            held, buffer = info, None
            sums, got = [{} for _ in pieces], [{} for _ in pieces]

            def send(p, step, block, *after):
                mine = sums[p][block]
                if step > 1:
                    mine = (mine.astype(F32) + got[p][step - 1, block].astype(F32)).astype(BF16)
                mine = tied(mine, *after) if after else mine
                lands = chan_count - 1 - block if step == half else block
                got[p][step, lands] = hop(step, mine)
                return mine

            def sent(step):
                return range(chan_count - 1, step - 1, -1) if step <= half else range(chan_count - step - 1, -1, -1)

            last = chan_count - 1
            for p, (first, size) in enumerate(pieces):
                mixed, sums[p][last] = project_first(first, size, held, operands)
                send(p, 1, last)
                held = tied(held, sums[p][last])
                rest = project_rest(size, held, mixed, weight)
                for k, block in enumerate(range(last - 1, -1, -1)):
                    sums[p][block] = rest[k]
                for block in range(last - 1, 0, -1):
                    send(p, 1, block)
                held = tied(held, rest[-1])
                if p + 1 < len(pieces):
                    held = tied(held, send(p, 2, last))
            def final(p, step):
                return got[p][step, step if step < half else chan_count - 1 - step]

            for p, (first, size) in enumerate(pieces):
                for step in range(2, chan_count):
                    for block in sent(step):
                        lands = chan_count - 1 - block if step == half else block
                        if (step, lands) not in got[p]:
                            ready = [final(p, k) for k in range(1, step)] if step > half and p + 1 < len(pieces) else []
                            send(p, step, block, *ready)
                own = [sums[p][k] for k in range(half)]
                mine = [final(p, step) for step in range(1, chan_count)]
                buffer = finish(first, size, buffer, own, mine)
            return buffer

        return run

    used = (length + (W - 1)) // W
    return lax.switch(used - 1, [branch(c + 1) for c in range(chunks)], (ut, qt, spread, enter, out_weight))


def solution(mesh):
    placed = (
        P(None, "chan", "ctx"),
        P(None, None, "chan"),
        P("ctx"),
        P("ctx"),
        P(None, "chan"),
        P(None, "chan"),
        P("chan"),
        P("chan", None),
    )
    body = functools.partial(shards, mesh.shape["chan"], mesh.shape["ctx"])
    return jax.shard_map(body, mesh=mesh, in_specs=placed, out_specs=P("chan", "ctx"), check_vma=False)
```

```python
import functools

import jax
import jax.numpy as jnp
from jax import lax
from jax.experimental import pallas as pl
from jax.experimental.pallas import tpu as pltpu
from jax.sharding import PartitionSpec as P

F32 = jnp.float32
BF16 = jnp.bfloat16
W = 128
CB = 128
MB = 1 << 20


def dot(a, b, dims, precision=None):
    return lax.dot_general(a, b, (dims, ((), ())), precision=precision, preferred_element_type=F32)


def iota(shape, axis):
    return lax.broadcasted_iota(jnp.int32, shape, axis)


def call(body, out_shape, grid, in_specs, out_specs, prefetch=0, scratch=(), aliases=None, flops=0, nbytes=0, exps=0, vmem=40, name=None):
    return pl.pallas_call(
        body,
        out_shape=out_shape,
        grid_spec=pltpu.PrefetchScalarGridSpec(
            num_scalar_prefetch=prefetch, grid=grid, in_specs=in_specs, out_specs=out_specs, scratch_shapes=list(scratch)
        ),
        input_output_aliases=aliases or {},
        cost_estimate=pl.CostEstimate(flops=flops, bytes_accessed=nbytes, transcendentals=exps),
        compiler_params=pltpu.CompilerParams(vmem_limit_bytes=vmem * MB),
        name=name,
    )


def rows_sum(x):
    return x[0] if len(x) == 1 else rows_sum(x[: len(x) // 2]) + rows_sum(x[len(x) // 2 :])


def tail_body(taps, width, info, near, every, out, far, sem):
    length = info[0]
    crossing = lax.rem(length - 1, W) == 0
    row, lane = iota((8, W), 0), iota((8, W), 1)

    def picked(src, places):
        acc = None
        for r in range(3):
            pick = functools.reduce(
                lambda x, y: x | y, [(row == r * (taps - 1) + k) & (lane == lax.rem(length - (taps - 1) + k, W)) for k in places]
            )
            term = dot(pick.astype(F32).astype(BF16), src[r], ((1,), (1,)))
            acc = term if acc is None else acc + term
        return acc

    @pl.when(jnp.logical_not(crossing))
    def _():
        out[...] = picked(near, range(taps - 1))

    @pl.when(crossing)
    def _():
        rows = pl.ds(pl.multiple_of(pl.program_id(0) * width, width), width)
        lanes = pl.ds(pl.multiple_of(lax.div(length - 2, W) * W, W), W)
        copy = pltpu.make_async_copy(every.at[:, rows, lanes], far, sem)
        copy.start()
        copy.wait()
        out[...] = picked(near, [taps - 2]) + picked(far, [taps - 3])


def set_tables(shift, spots, sets):
    col = iota((2 * W, 2 * W), 1)
    source = jnp.where(col < W, col + (W - 1), col - 2)
    shift[...] = (iota((2 * W, 2 * W), 0) == source).astype(F32).astype(BF16)
    row, lane = iota((W, W), 0), iota((W, W), 1)
    for n, r in enumerate(sets):
        for k in range(3):
            pick = (row == 3 * r + k) | (row == 16 + 3 * r + k)
            spots[:, (4 * n + k) * W : (4 * n + k + 1) * W] = pick.astype(F32).astype(BF16)
        pick = (row == lane - (W - 2) + 32 + 2 * r) & (lane >= W - 2)
        spots[:, (4 * n + 3) * W : (4 * n + 4) * W] = pick.astype(F32).astype(BF16)
    if 4 * len(sets) * W < spots.shape[1]:
        pick = (row == 9) | (row == 25)
        spots[:, 4 * len(sets) * W :] = pick.astype(F32).astype(BF16)


def turned(x):
    eye = (iota((W, W), 0) == iota((W, W), 1)).astype(F32).astype(BF16)
    return dot(eye, x, ((1,), (1,)))


def columns(par, halo, spots):
    high = par.astype(BF16).astype(F32)
    full = jnp.concatenate([high, par - high, halo, jnp.zeros((CB - 40, CB), F32)], axis=0).astype(BF16)
    return dot(turned(full).astype(BF16), spots, ((1,), (0,)))


def short_conv(block, cols, n, shift, first, chunks):
    w0, w1, w2, before = (cols[:, (4 * n + k) * W : (4 * n + k + 1) * W] for k in range(4))
    tiles = [block[:, j * W : (j + 1) * W] if j >= 0 else before.astype(BF16) for j in range(first - 1, first + chunks)]
    pairs = jnp.concatenate([jnp.concatenate(tiles[j : j + 2], axis=1) for j in range(chunks)], axis=0)
    moved = dot(pairs, shift, ((1,), (0,)))
    out = []
    for j in range(chunks):
        rows = slice(j * CB, (j + 1) * CB)
        out.append(w0 * tiles[j + 1].astype(F32) + w1 * moved[rows, :W] + w2 * moved[rows, W:])
    return out


def tiles_of(block, chunks):
    return [block[:, j * W : (j + 1) * W].astype(F32) for j in range(chunks)]


def product_body(chunks, steps, sub, info, k_ref, v_ref, halo, par, filters, p_ref, sq_ref, st_ref, shift, spots):
    i = pl.program_id(0)
    length, last_hi, last_lo = info[0], info[2], info[3]
    modes = sq_ref.shape[1]
    per = 8
    wide = CB // per * modes

    @pl.when(i == 0)
    def _():
        set_tables(shift, spots, (1, 2))

    def block(b, carry):
        rows = pl.ds(pl.multiple_of(b * CB, CB), CB)
        lane = iota((CB, W), 1)
        cols = columns(par[:, rows], halo[:, rows], spots[...])
        key = short_conv(k_ref[0, rows, :], cols, 0, shift[...], 0, chunks)
        val = short_conv(v_ref[0, rows, :], cols, 1, shift[...], 0, chunks)
        prod = [jnp.where(lane + j * W < length, key[j] * val[j], 0.0).astype(BF16) for j in range(chunks)]
        for j in range(chunks):
            p_ref[rows, j * W : (j + 1) * W] = prod[j]
        rate = filters[0, :, pl.ds(pl.multiple_of(b * wide, wide), wide)]
        slot = iota((W, wide), 0)
        ahead = jnp.exp(-rate * (W - slot).astype(F32)).astype(BF16)
        last_chunk = lax.div(length - 1, W)
        left = length - 1 - last_chunk * W - slot
        ending = jnp.where(left >= 0, jnp.exp(-rate * jnp.maximum(left, 0).astype(F32)), 0.0).astype(BF16)
        own = iota((CB, wide), 0) // per == iota((CB, wide), 1) // modes
        last = prod[0]
        for j in range(1, chunks):
            last = jnp.where(last_chunk == j, prod[j], last)
        fold = (lax.rem(iota((modes, wide), 1), modes) == iota((modes, wide), 0)).astype(F32).astype(BF16)
        total = dot(last, ending, ((1,), (0,)))
        every = dot(jnp.concatenate(prod, axis=0), ahead, ((1,), (0,)))
        for j in range(chunks):
            summary = every[j * CB : (j + 1) * CB]
            if j < chunks - 1:
                sq_ref[j, :, rows] = dot(fold, jnp.where(own, summary, 0.0).astype(BF16), ((1,), (1,)))
                rest = jnp.maximum(length - 1 - W * (j + 1), 0).astype(F32)
                total = total + jnp.where(j < last_chunk, jnp.exp(-rate * rest), 0.0) * summary
        ending_state = dot(fold, jnp.where(own, total, 0.0).astype(BF16), ((1,), (1,))).astype(BF16)
        for d in range(st_ref.shape[0]):
            st_ref[d, :, rows] = ending_state
        return carry

    @pl.when(i < steps)
    def _():
        lax.fori_loop(0, sub, block, 0, unroll=True)

    @pl.when(i == steps)
    def _():
        row = iota(st_ref.shape[1:], 0)
        mark = jnp.where(row == 0, last_hi, jnp.where(row == 1, last_lo, 0)).astype(F32).astype(BF16)
        for d in range(st_ref.shape[0]):
            st_ref[d] = mark


def rates_body(info, rates, rc_ref):
    groups, channels = rates.shape[1], rc_ref.shape[1]
    expand = (iota((groups, channels), 0) == iota((groups, channels), 1) // (channels // groups)).astype(F32)
    rc_ref[...] = dot(rates[...], expand, ((1,), (0,)), lax.Precision.HIGHEST)


def inner_body(chunks, sub, modes, info, q_ref, p_ref, halo, par, filters, *rest):
    ut_ref, qt_ref, sp_ref, shift, spots = rest[-5:]
    i = pl.program_id(0)
    length = info[0]
    per = 8
    groups = CB // per
    wide = groups * modes
    middle = W // 2

    @pl.when(i == 0)
    def _():
        set_tables(shift, spots, (0,))

    def block(b, carry):
        rows = pl.ds(pl.multiple_of(b * CB, CB), CB)
        lane = iota((CB, W), 1)
        cols = columns(par[:, rows], halo[:, rows], spots[...])
        query = short_conv(q_ref[0, rows, :], cols, 0, shift[...], 0, chunks)
        skip = cols[:, 4 * W : 5 * W]
        prod = tiles_of(p_ref[rows, :], chunks)
        at = pl.ds(pl.multiple_of(b * wide, wide), wide)
        rate, res = filters[0, :, at], filters[1, :, at]
        slot = iota((W, wide), 0).astype(F32)
        sp_ref[:, at] = (res * jnp.exp(-rate * slot)).astype(BF16)
        later = (res * jnp.exp(-rate * (slot - middle))).astype(BF16)
        sooner = jnp.exp(rate * (slot - middle)).astype(BF16)
        mine = iota((W, wide), 1) // modes
        upper = iota((W, W), 1) >= iota((W, W), 0)
        inner = [[] for _ in range(chunks)]
        kernels, stacks = [], []
        some = W // modes
        for h in range(groups // some):
            half = slice(h * W, h * W + W)
            left = jnp.concatenate(
                [jnp.where(mine[:, half] == h * some + g, sooner[:, half], jnp.zeros((W, W), BF16)) for g in range(some)], axis=0
            )
            full = dot(left, later[:, half], ((1,), (1,)))
            kernels += [jnp.where(upper, full[g * W : (g + 1) * W], 0.0).astype(BF16) for g in range(some)]
        for g in range(groups):
            stacks.append(jnp.concatenate([prod[j][g * per : (g + 1) * per] for j in range(chunks)], axis=0).astype(BF16))
        for g in range(groups):
            result = dot(stacks[g], kernels[g], ((1,), (0,)))
            for j in range(chunks):
                inner[j].append(result[j * per : (j + 1) * per])
        for j in range(chunks):
            used = lane + j * W < length
            q = jnp.where(used, query[j], 0.0)
            u = q * (jnp.concatenate(inner[j], axis=0) + skip * prod[j])
            ut_ref[j * W : (j + 1) * W, rows] = jnp.transpose(u.astype(BF16))
            qt_ref[j * W : (j + 1) * W, rows] = jnp.transpose(q.astype(BF16))
        return carry

    lax.fori_loop(0, sub, block, 0, unroll=2)


def enter_body(chunks, info, every, rc, sq, e_ref):
    first = info[1].astype(F32)
    channels = rc.shape[1]
    rate = rc[...]

    def shard(i, state):
        mark = every[i, 0:2, channels : channels + 128].astype(F32)
        gap = first - (mark[0:1, 0:1] * 256.0 + mark[1:2, 0:1])
        came = jnp.exp(-rate * jnp.maximum(gap, 0.0)) * every[i, :, 0:channels].astype(F32)
        return state + jnp.where(i < info[6], came, 0.0)

    state = jnp.zeros(rate.shape, F32)
    for i in range(every.shape[0] - 1):
        state = shard(i, state)
    over = jnp.exp(-rate * float(W))
    for j in range(chunks):
        e_ref[j] = state.astype(BF16)
        if j < chunks - 1:
            state = over * state + sq[j]


def project_first_body(sub, info, ut, qt, sp, e_ref, w_ref, m_ref, out, acc):
    k = pl.program_id(0)
    count, modes = e_ref.shape[:2]
    per = 8
    groups = CB // per
    own = iota((groups * modes, CB), 0) // modes == iota((groups * modes, CB), 1) // per
    own = own.astype(F32).astype(BF16)
    for b in range(sub):
        at = slice(b * CB, (b + 1) * CB)
        diagonal = [own * jnp.concatenate([e_ref[c, :, at]] * groups, axis=0) for c in range(count)]
        spread = sp[:, b * groups * modes : (b + 1) * groups * modes]
        outer = dot(spread, jnp.concatenate(diagonal, axis=1), ((1,), (0,)))
        for c in range(count):
            rows = slice(c * W, (c + 1) * W)
            gate = qt[rows, at].astype(F32) * outer[:, c * CB : (c + 1) * CB]
            m_ref[rows, at] = (ut[rows, at].astype(F32) + gate).astype(BF16)
    term = dot(m_ref[...], w_ref[...], ((1,), (0,)))

    @pl.when(k == 0)
    def _():
        acc[...] = term

    @pl.when(k > 0)
    def _():
        acc[...] += term

    @pl.when(k == pl.num_programs(0) - 1)
    def _():
        out[...] = acc[...].astype(BF16)


def project_rest_body(per_out, info, m_ref, w_ref, *outs):
    i = pl.program_id(0)
    for k, out in enumerate(outs):

        @pl.when(i // per_out == k)
        def _(out=out):
            out[...] = dot(m_ref[...], w_ref[...], ((1,), (0,))).astype(BF16)


def finish_body(owns, fresh, rows, info, *refs):
    acc = refs[0][...].astype(F32)
    for k in range(1, owns):
        acc = jnp.where(info[5] == k, refs[k][...].astype(F32), acc)
    for ref in refs[owns : len(refs) - 1 - (not fresh)]:
        acc = acc + ref[...].astype(F32)
    out = refs[-1]
    done = jnp.transpose(acc).astype(BF16)
    if out.shape[1] > rows:
        out[:, :rows] = done
        out[:, rows:] = jnp.zeros((out.shape[0], out.shape[1] - rows), BF16)
    else:
        out[...] = done


def shards(chan_count, ctx_count, features, short_filter, lengths, offsets, decay_rates, residues, skip_weight, out_weight):
    taps = short_filter.shape[1]
    channels, slots = features.shape[1], features.shape[2]
    modes, groups = decay_rates.shape
    out_width = out_weight.shape[1]
    chunks = slots // W
    blocks = channels // CB
    per_block = groups // blocks
    length, offset = lengths[0], offsets[0]
    rank = lax.axis_index("chan")
    flip = (rank >= chan_count // 2).astype(jnp.int32)
    depth = jnp.minimum(rank, chan_count - 1 - rank).astype(jnp.int32)
    last = offset + length - 1
    shard = lax.axis_index("ctx")
    info = jnp.stack([length, offset, last // 256, last % 256, flip, depth, shard.astype(jnp.int32)])
    par = jnp.concatenate(
        [short_filter.reshape(3 * taps, channels), skip_weight[None], jnp.zeros((6, channels), F32)], axis=0
    )

    tail_width = 1024
    tail = call(
        functools.partial(tail_body, taps, tail_width),
        jax.ShapeDtypeStruct((8, channels), F32),
        (channels // tail_width,),
        [
            pl.BlockSpec((3, tail_width, W), lambda i, s: (0, i, lax.div(s[0] - 1, W))),
            pl.BlockSpec(memory_space=pl.ANY),
        ],
        pl.BlockSpec((8, tail_width), lambda i, s: (0, i)),
        prefetch=1,
        scratch=[pltpu.VMEM((3, tail_width, W), BF16), pltpu.SemaphoreType.DMA],
        nbytes=6 * channels * W,
        vmem=60,
        name="tail",
    )(info, features, features)
    halo = lax.ppermute(tail, "ctx", [(i, i + 1) for i in range(ctx_count - 1)])

    rows = jnp.transpose(jnp.stack([decay_rates, residues]), (0, 2, 1)).reshape(2, 1, groups * modes)
    sub = 4
    step_channels = sub * CB
    steps = channels // step_channels
    inside = lambda i: jnp.minimum(i, steps - 1)
    tables = lambda sets, extra: [pltpu.VMEM((2 * W, 2 * W), BF16), pltpu.VMEM((W, (4 * sets + extra) * W), BF16)]
    whole = lambda shape: pl.BlockSpec(shape, lambda i, s: (0,) * len(shape))
    rate_ch = call(
        rates_body,
        jax.ShapeDtypeStruct((modes, channels), F32),
        (1,),
        [whole((modes, groups))],
        whole((modes, channels)),
        prefetch=1,
        nbytes=4 * modes * channels,
        vmem=60,
        name="rates",
    )(info, decay_rates)
    halo, _ = lax.optimization_barrier((halo, rate_ch))
    prod, sums, ends = call(
        functools.partial(product_body, chunks, steps, sub),
        (
            jax.ShapeDtypeStruct((channels, slots), BF16),
            jax.ShapeDtypeStruct((chunks - 1, modes, channels), F32),
            jax.ShapeDtypeStruct((ctx_count, modes, channels + 128), BF16),
        ),
        (steps + 1,),
        [
            pl.BlockSpec((1, step_channels, slots), lambda i, s: (1, inside(i), 0)),
            pl.BlockSpec((1, step_channels, slots), lambda i, s: (2, inside(i), 0)),
            pl.BlockSpec((8, step_channels), lambda i, s: (0, inside(i))),
            pl.BlockSpec((16, step_channels), lambda i, s: (0, inside(i))),
            pl.BlockSpec((1, 1, sub * per_block * modes), lambda i, s: (0, 0, inside(i))),
        ],
        (
            pl.BlockSpec((step_channels, slots), lambda i, s: (inside(i), 0)),
            pl.BlockSpec((chunks - 1, modes, step_channels), lambda i, s: (0, 0, inside(i))),
            pl.BlockSpec((ctx_count, modes, step_channels), lambda i, s: (0, 0, i)),
        ),
        prefetch=1,
        scratch=tables(2, 0),
        flops=20 * channels * slots,
        nbytes=6 * channels * slots,
        exps=modes * groups * 2 * W,
        vmem=60,
        name="product",
    )(info, features, features, halo, par, rows)
    every = lax.all_to_all(ends, "ctx", split_axis=0, concat_axis=0, tiled=True)
    wide = sub * per_block * modes

    def inner(first, count, info, before):
        at = lambda i: i + first
        return call(
            functools.partial(inner_body, chunks, sub, modes),
            (
                jax.ShapeDtypeStruct((slots, channels), BF16),
                jax.ShapeDtypeStruct((slots, channels), BF16),
                jax.ShapeDtypeStruct((W, groups * modes), BF16),
            ),
            (count,),
            [
                pl.BlockSpec((1, step_channels, slots), lambda i, s: (0, at(i), 0)),
                pl.BlockSpec((step_channels, slots), lambda i, s: (at(i), 0)),
                pl.BlockSpec((8, step_channels), lambda i, s: (0, at(i))),
                pl.BlockSpec((16, step_channels), lambda i, s: (0, at(i))),
                pl.BlockSpec((2, 1, wide), lambda i, s: (0, 0, at(i))),
            ]
            + [pl.BlockSpec(memory_space=pl.ANY)] * len(before),
            (
                pl.BlockSpec((slots, step_channels), lambda i, s: (0, at(i))),
                pl.BlockSpec((slots, step_channels), lambda i, s: (0, at(i))),
                pl.BlockSpec((W, wide), lambda i, s: (0, at(i))),
            ),
            prefetch=1,
            scratch=tables(1, 1),
            aliases={6 + k: k for k in range(len(before))},
            flops=2 * count * step_channels * slots * W,
            nbytes=8 * count * step_channels * slots,
            exps=3 * modes * groups * W * count // steps,
            vmem=60,
            name="inner",
        )(info, features, prod, halo, par, rows, *before)

    ut, qt, spread = inner(0, steps, info, ())

    lead = min(2, chunks)
    enter = call(
        functools.partial(enter_body, chunks),
        jax.ShapeDtypeStruct((chunks, modes, channels), BF16),
        (1,),
        [whole(every.shape), whole((modes, channels)), whole((chunks - 1, modes, channels))],
        whole((chunks, modes, channels)),
        prefetch=1,
        nbytes=8 * modes * channels * 2,
        exps=8 * modes * channels,
        vmem=60,
        name="enter",
    )(info, every, rate_ch, sums)

    half = chan_count // 2
    block_width = out_width // chan_count
    tile = min(1024, block_width)
    per_out = block_width // tile

    def column(block, sub, s):
        return jnp.where(s[4] == 0, block, chan_count - 1 - block) * per_out + sub

    def project_first(first, count, info, operands):
        ut, qt, spread, enter, weight = operands
        return call(
            functools.partial(project_first_body, sub),
            (jax.ShapeDtypeStruct((count * W, channels), BF16), jax.ShapeDtypeStruct((count * W, block_width), BF16)),
            (steps,),
            [
                pl.BlockSpec((count * W, step_channels), lambda i, s: (first // count, i)),
                pl.BlockSpec((count * W, step_channels), lambda i, s: (first // count, i)),
                pl.BlockSpec((W, wide), lambda i, s: (0, i)),
                pl.BlockSpec((count, modes, step_channels), lambda i, s: (first // count, 0, i)),
                pl.BlockSpec((step_channels, block_width), lambda i, s: (i, jnp.where(s[4] == 0, chan_count - 1, 0))),
            ],
            (
                pl.BlockSpec((count * W, step_channels), lambda i, s: (0, i)),
                pl.BlockSpec((count * W, block_width), lambda i, s: (0, 0)),
            ),
            prefetch=1,
            scratch=[pltpu.VMEM((count * W, block_width), F32)],
            flops=2 * count * W * channels * (block_width + modes * CB // 8),
            nbytes=2 * channels * (block_width + 4 * count * W),
            vmem=60,
            name="project_first",
        )(info, ut, qt, spread, enter, weight)

    def project_rest(count, info, mixed, weight):
        number = chan_count - 1
        return call(
            functools.partial(project_rest_body, per_out),
            [jax.ShapeDtypeStruct((count * W, block_width), BF16)] * number,
            (number * per_out,),
            [
                pl.BlockSpec((count * W, channels), lambda i, s: (0, 0)),
                pl.BlockSpec((channels, tile), lambda i, s: (0, column(number - 1 - i // per_out, lax.rem(i, per_out), s))),
            ],
            [
                pl.BlockSpec((count * W, tile), lambda i, s, k=k: (0, jnp.clip(i - k * per_out, 0, per_out - 1)))
                for k in range(number)
            ],
            prefetch=1,
            flops=2 * count * W * channels * number * block_width,
            nbytes=2 * channels * number * block_width,
            vmem=60,
            name="project_rest",
        )(info, mixed, weight)

    def finish(first, count, buffer, own, parts):
        fresh = buffer is None
        rows = count * W
        specs = [pl.BlockSpec((rows, block_width), lambda i, s: (0, 0))] * (len(own) + len(parts))
        arrays = [*own, *parts]
        if not fresh:
            specs = specs + [pl.BlockSpec(memory_space=pl.ANY)]
            arrays.append(buffer)
        return call(
            functools.partial(finish_body, len(own), fresh, rows),
            jax.ShapeDtypeStruct((block_width, slots), BF16),
            (1,),
            specs,
            pl.BlockSpec((block_width, slots if fresh else rows), lambda i, s: (0, 0 if fresh else first // count)),
            prefetch=1,
            aliases=None if fresh else {len(arrays): 0},
            nbytes=(len(parts) + 2) * rows * block_width * 2,
            name="finish",
        )(info, *arrays)

    def hop(step, array):
        return lax.ppermute(array, "chan", [(step - 1, step), (chan_count - step, chan_count - step - 1)])

    def tied(value, *after):
        return lax.optimization_barrier((value, *after))[0]

    def branch(count):
        pieces = [(first, min(lead, count - first)) for first in range(0, count, lead)]

        def run(operands):
            weight = operands[-1]
            held, buffer = info, None
            sums, got = [{} for _ in pieces], [{} for _ in pieces]

            def send(p, step, block, *after):
                mine = sums[p][block]
                if step > 1:
                    mine = (mine.astype(F32) + got[p][step - 1, block].astype(F32)).astype(BF16)
                mine = tied(mine, *after) if after else mine
                lands = chan_count - 1 - block if step == half else block
                got[p][step, lands] = hop(step, mine)
                return mine

            def sent(step):
                return range(chan_count - 1, step - 1, -1) if step <= half else range(chan_count - step - 1, -1, -1)

            last = chan_count - 1
            for p, (first, size) in enumerate(pieces):
                mixed, sums[p][last] = project_first(first, size, held, operands)
                send(p, 1, last)
                held = tied(held, sums[p][last])
                rest = project_rest(size, held, mixed, weight)
                for k, block in enumerate(range(last - 1, -1, -1)):
                    sums[p][block] = rest[k]
                for block in range(last - 1, 0, -1):
                    send(p, 1, block)
                held = tied(held, rest[-1])
                if p + 1 < len(pieces):
                    held = tied(held, send(p, 2, last))
            def final(p, step):
                return got[p][step, step if step < half else chan_count - 1 - step]

            for p, (first, size) in enumerate(pieces):
                for step in range(2, chan_count):
                    for block in sent(step):
                        lands = chan_count - 1 - block if step == half else block
                        if (step, lands) not in got[p]:
                            ready = [final(p, k) for k in range(1, step)] if step > half and p + 1 < len(pieces) else []
                            send(p, step, block, *ready)
                own = [sums[p][k] for k in range(half)]
                mine = [final(p, step) for step in range(1, chan_count)]
                buffer = finish(first, size, buffer, own, mine)
            return buffer

        return run

    used = (length + (W - 1)) // W
    return lax.switch(used - 1, [branch(c + 1) for c in range(chunks)], (ut, qt, spread, enter, out_weight))


def solution(mesh):
    placed = (
        P(None, "chan", "ctx"),
        P(None, None, "chan"),
        P("ctx"),
        P("ctx"),
        P(None, "chan"),
        P(None, "chan"),
        P("chan"),
        P("chan", None),
    )
    body = functools.partial(shards, mesh.shape["chan"], mesh.shape["ctx"])
    return jax.shard_map(body, mesh=mesh, in_specs=placed, out_specs=P("chan", "ctx"), check_vma=False)
```

```python
import functools

import jax
import jax.numpy as jnp
from jax import lax
from jax.experimental import pallas as pl
from jax.experimental.pallas import tpu as pltpu
from jax.sharding import PartitionSpec as P

F32 = jnp.float32
BF16 = jnp.bfloat16
W = 128
CB = 128
MB = 1 << 20


def dot(a, b, dims, precision=None):
    return lax.dot_general(a, b, (dims, ((), ())), precision=precision, preferred_element_type=F32)


def iota(shape, axis):
    return lax.broadcasted_iota(jnp.int32, shape, axis)


def call(body, out_shape, grid, in_specs, out_specs, prefetch=0, scratch=(), aliases=None, flops=0, nbytes=0, exps=0, vmem=40, name=None):
    return pl.pallas_call(
        body,
        out_shape=out_shape,
        grid_spec=pltpu.PrefetchScalarGridSpec(
            num_scalar_prefetch=prefetch, grid=grid, in_specs=in_specs, out_specs=out_specs, scratch_shapes=list(scratch)
        ),
        input_output_aliases=aliases or {},
        cost_estimate=pl.CostEstimate(flops=flops, bytes_accessed=nbytes, transcendentals=exps),
        compiler_params=pltpu.CompilerParams(vmem_limit_bytes=vmem * MB),
        name=name,
    )


def rows_sum(x):
    return x[0] if len(x) == 1 else rows_sum(x[: len(x) // 2]) + rows_sum(x[len(x) // 2 :])


def tail_body(taps, width, info, near, every, out, far, sem):
    length = info[0]
    crossing = lax.rem(length - 1, W) == 0
    row, lane = iota((8, W), 0), iota((8, W), 1)

    def picked(src, places):
        acc = None
        for r in range(3):
            pick = functools.reduce(
                lambda x, y: x | y, [(row == r * (taps - 1) + k) & (lane == lax.rem(length - (taps - 1) + k, W)) for k in places]
            )
            term = dot(pick.astype(F32).astype(BF16), src[r], ((1,), (1,)))
            acc = term if acc is None else acc + term
        return acc

    @pl.when(jnp.logical_not(crossing))
    def _():
        out[...] = picked(near, range(taps - 1))

    @pl.when(crossing)
    def _():
        rows = pl.ds(pl.multiple_of(pl.program_id(0) * width, width), width)
        lanes = pl.ds(pl.multiple_of(lax.div(length - 2, W) * W, W), W)
        copy = pltpu.make_async_copy(every.at[:, rows, lanes], far, sem)
        copy.start()
        copy.wait()
        out[...] = picked(near, [taps - 2]) + picked(far, [taps - 3])


def set_tables(shift, spots, sets):
    col = iota((2 * W, 2 * W), 1)
    source = jnp.where(col < W, col + (W - 1), col - 2)
    shift[...] = (iota((2 * W, 2 * W), 0) == source).astype(F32).astype(BF16)
    row, lane = iota((W, W), 0), iota((W, W), 1)
    for n, r in enumerate(sets):
        for k in range(3):
            pick = (row == 3 * r + k) | (row == 16 + 3 * r + k)
            spots[:, (4 * n + k) * W : (4 * n + k + 1) * W] = pick.astype(F32).astype(BF16)
        pick = (row == lane - (W - 2) + 32 + 2 * r) & (lane >= W - 2)
        spots[:, (4 * n + 3) * W : (4 * n + 4) * W] = pick.astype(F32).astype(BF16)
    if 4 * len(sets) * W < spots.shape[1]:
        pick = (row == 9) | (row == 25)
        spots[:, 4 * len(sets) * W :] = pick.astype(F32).astype(BF16)


def turned(x):
    eye = (iota((W, W), 0) == iota((W, W), 1)).astype(F32).astype(BF16)
    return dot(eye, x, ((1,), (1,)))


def columns(par, halo, spots):
    high = par.astype(BF16).astype(F32)
    full = jnp.concatenate([high, par - high, halo, jnp.zeros((CB - 40, CB), F32)], axis=0).astype(BF16)
    return dot(turned(full).astype(BF16), spots, ((1,), (0,)))


def short_conv(block, cols, n, shift, first, chunks):
    w0, w1, w2, before = (cols[:, (4 * n + k) * W : (4 * n + k + 1) * W] for k in range(4))
    tiles = [block[:, j * W : (j + 1) * W] if j >= 0 else before.astype(BF16) for j in range(first - 1, first + chunks)]
    pairs = jnp.concatenate([jnp.concatenate(tiles[j : j + 2], axis=1) for j in range(chunks)], axis=0)
    moved = dot(pairs, shift, ((1,), (0,)))
    out = []
    for j in range(chunks):
        rows = slice(j * CB, (j + 1) * CB)
        out.append(w0 * tiles[j + 1].astype(F32) + w1 * moved[rows, :W] + w2 * moved[rows, W:])
    return out


def tiles_of(block, chunks):
    return [block[:, j * W : (j + 1) * W].astype(F32) for j in range(chunks)]


def product_body(chunks, steps, sub, info, k_ref, v_ref, halo, par, filters, p_ref, sq_ref, st_ref, shift, spots):
    i = pl.program_id(0)
    length, last_hi, last_lo = info[0], info[2], info[3]
    modes = sq_ref.shape[1]
    per = 8
    wide = CB // per * modes

    @pl.when(i == 0)
    def _():
        set_tables(shift, spots, (1, 2))

    def block(b, carry):
        rows = pl.ds(pl.multiple_of(b * CB, CB), CB)
        lane = iota((CB, W), 1)
        cols = columns(par[:, rows], halo[:, rows], spots[...])
        key = short_conv(k_ref[0, rows, :], cols, 0, shift[...], 0, chunks)
        val = short_conv(v_ref[0, rows, :], cols, 1, shift[...], 0, chunks)
        prod = [jnp.where(lane + j * W < length, key[j] * val[j], 0.0).astype(BF16) for j in range(chunks)]
        for j in range(chunks):
            p_ref[rows, j * W : (j + 1) * W] = prod[j]
        rate = filters[0, :, pl.ds(pl.multiple_of(b * wide, wide), wide)]
        slot = iota((W, wide), 0)
        ahead = jnp.exp(-rate * (W - slot).astype(F32)).astype(BF16)
        last_chunk = lax.div(length - 1, W)
        left = length - 1 - last_chunk * W - slot
        ending = jnp.where(left >= 0, jnp.exp(-rate * jnp.maximum(left, 0).astype(F32)), 0.0).astype(BF16)
        own = iota((CB, wide), 0) // per == iota((CB, wide), 1) // modes
        last = prod[0]
        for j in range(1, chunks):
            last = jnp.where(last_chunk == j, prod[j], last)
        fold = (lax.rem(iota((modes, wide), 1), modes) == iota((modes, wide), 0)).astype(F32).astype(BF16)
        total = dot(last, ending, ((1,), (0,)))
        every = dot(jnp.concatenate(prod, axis=0), ahead, ((1,), (0,)))
        for j in range(chunks):
            summary = every[j * CB : (j + 1) * CB]
            if j < chunks - 1:
                sq_ref[j, :, rows] = dot(fold, jnp.where(own, summary, 0.0).astype(BF16), ((1,), (1,)))
                rest = jnp.maximum(length - 1 - W * (j + 1), 0).astype(F32)
                total = total + jnp.where(j < last_chunk, jnp.exp(-rate * rest), 0.0) * summary
        ending_state = dot(fold, jnp.where(own, total, 0.0).astype(BF16), ((1,), (1,))).astype(BF16)
        for d in range(st_ref.shape[0]):
            st_ref[d, :, rows] = ending_state
        return carry

    @pl.when(i < steps)
    def _():
        lax.fori_loop(0, sub, block, 0, unroll=True)

    @pl.when(i == steps)
    def _():
        row = iota(st_ref.shape[1:], 0)
        mark = jnp.where(row == 0, last_hi, jnp.where(row == 1, last_lo, 0)).astype(F32).astype(BF16)
        for d in range(st_ref.shape[0]):
            st_ref[d] = mark


def rates_body(info, rates, rc_ref):
    groups, channels = rates.shape[1], rc_ref.shape[1]
    expand = (iota((groups, channels), 0) == iota((groups, channels), 1) // (channels // groups)).astype(F32)
    rc_ref[...] = dot(rates[...], expand, ((1,), (0,)), lax.Precision.HIGHEST)


def inner_body(chunks, sub, modes, info, q_ref, p_ref, halo, par, filters, *rest):
    ut_ref, qt_ref, sp_ref, shift, spots = rest[-5:]
    i = pl.program_id(0)
    length = info[0]
    per = 8
    groups = CB // per
    wide = groups * modes
    middle = W // 2

    @pl.when(i == 0)
    def _():
        set_tables(shift, spots, (0,))

    def block(b, carry):
        rows = pl.ds(pl.multiple_of(b * CB, CB), CB)
        lane = iota((CB, W), 1)
        cols = columns(par[:, rows], halo[:, rows], spots[...])
        query = short_conv(q_ref[0, rows, :], cols, 0, shift[...], 0, chunks)
        skip = cols[:, 4 * W : 5 * W]
        prod = tiles_of(p_ref[rows, :], chunks)
        at = pl.ds(pl.multiple_of(b * wide, wide), wide)
        rate, res = filters[0, :, at], filters[1, :, at]
        slot = iota((W, wide), 0).astype(F32)
        sp_ref[:, at] = (res * jnp.exp(-rate * slot)).astype(BF16)
        later = (res * jnp.exp(-rate * (slot - middle))).astype(BF16)
        sooner = jnp.exp(rate * (slot - middle)).astype(BF16)
        mine = iota((W, wide), 1) // modes
        upper = iota((W, W), 1) >= iota((W, W), 0)
        inner = [[] for _ in range(chunks)]
        kernels, stacks = [], []
        some = W // modes
        for h in range(groups // some):
            half = slice(h * W, h * W + W)
            left = jnp.concatenate(
                [jnp.where(mine[:, half] == h * some + g, sooner[:, half], jnp.zeros((W, W), BF16)) for g in range(some)], axis=0
            )
            full = dot(left, later[:, half], ((1,), (1,)))
            kernels += [jnp.where(upper, full[g * W : (g + 1) * W], 0.0).astype(BF16) for g in range(some)]
        for g in range(groups):
            stacks.append(jnp.concatenate([prod[j][g * per : (g + 1) * per] for j in range(chunks)], axis=0).astype(BF16))
        for g in range(groups):
            result = dot(stacks[g], kernels[g], ((1,), (0,)))
            for j in range(chunks):
                inner[j].append(result[j * per : (j + 1) * per])
        for j in range(chunks):
            used = lane + j * W < length
            q = jnp.where(used, query[j], 0.0)
            u = q * (jnp.concatenate(inner[j], axis=0) + skip * prod[j])
            ut_ref[j * W : (j + 1) * W, rows] = jnp.transpose(u.astype(BF16))
            qt_ref[j * W : (j + 1) * W, rows] = jnp.transpose(q.astype(BF16))
        return carry

    lax.fori_loop(0, sub, block, 0, unroll=2)


def enter_body(chunks, info, every, rc, sq, e_ref):
    first = info[1].astype(F32)
    channels = rc.shape[1]
    rate = rc[...]

    def shard(i, state):
        mark = every[i, 0:2, channels : channels + 128].astype(F32)
        gap = first - (mark[0:1, 0:1] * 256.0 + mark[1:2, 0:1])
        came = jnp.exp(-rate * jnp.maximum(gap, 0.0)) * every[i, :, 0:channels].astype(F32)
        return state + jnp.where(i < info[6], came, 0.0)

    state = jnp.zeros(rate.shape, F32)
    for i in range(every.shape[0] - 1):
        state = shard(i, state)
    over = jnp.exp(-rate * float(W))
    for j in range(chunks):
        e_ref[j] = state.astype(BF16)
        if j < chunks - 1:
            state = over * state + sq[j]


def project_first_body(sub, info, ut, qt, sp, e_ref, w_ref, m_ref, out, acc):
    k = pl.program_id(0)
    count, modes = e_ref.shape[:2]
    per = 8
    groups = CB // per
    own = iota((groups * modes, CB), 0) // modes == iota((groups * modes, CB), 1) // per
    own = own.astype(F32).astype(BF16)
    for b in range(sub):
        at = slice(b * CB, (b + 1) * CB)
        diagonal = [own * jnp.concatenate([e_ref[c, :, at]] * groups, axis=0) for c in range(count)]
        spread = sp[:, b * groups * modes : (b + 1) * groups * modes]
        outer = dot(spread, jnp.concatenate(diagonal, axis=1), ((1,), (0,)))
        for c in range(count):
            rows = slice(c * W, (c + 1) * W)
            gate = qt[rows, at].astype(F32) * outer[:, c * CB : (c + 1) * CB]
            m_ref[rows, at] = (ut[rows, at].astype(F32) + gate).astype(BF16)
    term = dot(m_ref[...], w_ref[...], ((1,), (0,)))

    @pl.when(k == 0)
    def _():
        acc[...] = term

    @pl.when(k > 0)
    def _():
        acc[...] += term

    @pl.when(k == pl.num_programs(0) - 1)
    def _():
        out[...] = acc[...].astype(BF16)


def project_rest_body(starts, info, m_ref, w_ref, *outs):
    i = pl.program_id(0)
    for k, out in enumerate(outs):

        @pl.when((i >= starts[k]) & (i < starts[k + 1]))
        def _(out=out):
            out[...] = dot(m_ref[...], w_ref[...], ((1,), (0,))).astype(BF16)


def finish_body(owns, fresh, rows, info, *refs):
    acc = refs[0][...].astype(F32)
    for k in range(1, owns):
        acc = jnp.where(info[5] == k, refs[k][...].astype(F32), acc)
    for ref in refs[owns : len(refs) - 1 - (not fresh)]:
        acc = acc + ref[...].astype(F32)
    out = refs[-1]
    done = jnp.transpose(acc).astype(BF16)
    if out.shape[1] > rows:
        out[:, :rows] = done
        out[:, rows:] = jnp.zeros((out.shape[0], out.shape[1] - rows), BF16)
    else:
        out[...] = done


def shards(chan_count, ctx_count, features, short_filter, lengths, offsets, decay_rates, residues, skip_weight, out_weight):
    taps = short_filter.shape[1]
    channels, slots = features.shape[1], features.shape[2]
    modes, groups = decay_rates.shape
    out_width = out_weight.shape[1]
    chunks = slots // W
    blocks = channels // CB
    per_block = groups // blocks
    length, offset = lengths[0], offsets[0]
    rank = lax.axis_index("chan")
    flip = (rank >= chan_count // 2).astype(jnp.int32)
    depth = jnp.minimum(rank, chan_count - 1 - rank).astype(jnp.int32)
    last = offset + length - 1
    shard = lax.axis_index("ctx")
    info = jnp.stack([length, offset, last // 256, last % 256, flip, depth, shard.astype(jnp.int32)])
    par = jnp.concatenate(
        [short_filter.reshape(3 * taps, channels), skip_weight[None], jnp.zeros((6, channels), F32)], axis=0
    )

    tail_width = 1024
    tail = call(
        functools.partial(tail_body, taps, tail_width),
        jax.ShapeDtypeStruct((8, channels), F32),
        (channels // tail_width,),
        [
            pl.BlockSpec((3, tail_width, W), lambda i, s: (0, i, lax.div(s[0] - 1, W))),
            pl.BlockSpec(memory_space=pl.ANY),
        ],
        pl.BlockSpec((8, tail_width), lambda i, s: (0, i)),
        prefetch=1,
        scratch=[pltpu.VMEM((3, tail_width, W), BF16), pltpu.SemaphoreType.DMA],
        nbytes=6 * channels * W,
        vmem=60,
        name="tail",
    )(info, features, features)
    halo = lax.ppermute(tail, "ctx", [(i, i + 1) for i in range(ctx_count - 1)])

    rows = jnp.transpose(jnp.stack([decay_rates, residues]), (0, 2, 1)).reshape(2, 1, groups * modes)
    sub = 4
    step_channels = sub * CB
    steps = channels // step_channels
    inside = lambda i: jnp.minimum(i, steps - 1)
    tables = lambda sets, extra: [pltpu.VMEM((2 * W, 2 * W), BF16), pltpu.VMEM((W, (4 * sets + extra) * W), BF16)]
    whole = lambda shape: pl.BlockSpec(shape, lambda i, s: (0,) * len(shape))
    rate_ch = call(
        rates_body,
        jax.ShapeDtypeStruct((modes, channels), F32),
        (1,),
        [whole((modes, groups))],
        whole((modes, channels)),
        prefetch=1,
        nbytes=4 * modes * channels,
        vmem=60,
        name="rates",
    )(info, decay_rates)
    halo, _ = lax.optimization_barrier((halo, rate_ch))
    prod, sums, ends = call(
        functools.partial(product_body, chunks, steps, sub),
        (
            jax.ShapeDtypeStruct((channels, slots), BF16),
            jax.ShapeDtypeStruct((chunks - 1, modes, channels), F32),
            jax.ShapeDtypeStruct((ctx_count, modes, channels + 128), BF16),
        ),
        (steps + 1,),
        [
            pl.BlockSpec((1, step_channels, slots), lambda i, s: (1, inside(i), 0)),
            pl.BlockSpec((1, step_channels, slots), lambda i, s: (2, inside(i), 0)),
            pl.BlockSpec((8, step_channels), lambda i, s: (0, inside(i))),
            pl.BlockSpec((16, step_channels), lambda i, s: (0, inside(i))),
            pl.BlockSpec((1, 1, sub * per_block * modes), lambda i, s: (0, 0, inside(i))),
        ],
        (
            pl.BlockSpec((step_channels, slots), lambda i, s: (inside(i), 0)),
            pl.BlockSpec((chunks - 1, modes, step_channels), lambda i, s: (0, 0, inside(i))),
            pl.BlockSpec((ctx_count, modes, step_channels), lambda i, s: (0, 0, i)),
        ),
        prefetch=1,
        scratch=tables(2, 0),
        flops=20 * channels * slots,
        nbytes=6 * channels * slots,
        exps=modes * groups * 2 * W,
        vmem=60,
        name="product",
    )(info, features, features, halo, par, rows)
    every = lax.all_to_all(ends, "ctx", split_axis=0, concat_axis=0, tiled=True)
    wide = sub * per_block * modes

    def inner(first, count, info, before):
        at = lambda i: i + first
        return call(
            functools.partial(inner_body, chunks, sub, modes),
            (
                jax.ShapeDtypeStruct((slots, channels), BF16),
                jax.ShapeDtypeStruct((slots, channels), BF16),
                jax.ShapeDtypeStruct((W, groups * modes), BF16),
            ),
            (count,),
            [
                pl.BlockSpec((1, step_channels, slots), lambda i, s: (0, at(i), 0)),
                pl.BlockSpec((step_channels, slots), lambda i, s: (at(i), 0)),
                pl.BlockSpec((8, step_channels), lambda i, s: (0, at(i))),
                pl.BlockSpec((16, step_channels), lambda i, s: (0, at(i))),
                pl.BlockSpec((2, 1, wide), lambda i, s: (0, 0, at(i))),
            ]
            + [pl.BlockSpec(memory_space=pl.ANY)] * len(before),
            (
                pl.BlockSpec((slots, step_channels), lambda i, s: (0, at(i))),
                pl.BlockSpec((slots, step_channels), lambda i, s: (0, at(i))),
                pl.BlockSpec((W, wide), lambda i, s: (0, at(i))),
            ),
            prefetch=1,
            scratch=tables(1, 1),
            aliases={6 + k: k for k in range(len(before))},
            flops=2 * count * step_channels * slots * W,
            nbytes=8 * count * step_channels * slots,
            exps=3 * modes * groups * W * count // steps,
            vmem=60,
            name="inner",
        )(info, features, prod, halo, par, rows, *before)

    ut, qt, spread = inner(0, steps, info, ())

    lead = min(2, chunks)
    enter = call(
        functools.partial(enter_body, chunks),
        jax.ShapeDtypeStruct((chunks, modes, channels), BF16),
        (1,),
        [whole(every.shape), whole((modes, channels)), whole((chunks - 1, modes, channels))],
        whole((chunks, modes, channels)),
        prefetch=1,
        nbytes=8 * modes * channels * 2,
        exps=8 * modes * channels,
        vmem=60,
        name="enter",
    )(info, every, rate_ch, sums)

    half = chan_count // 2
    block_width = out_width // chan_count
    tile = min(1024, block_width)
    per_out = block_width // tile

    def column(block, sub, s):
        return jnp.where(s[4] == 0, block, chan_count - 1 - block) * per_out + sub

    def project_first(first, count, info, operands):
        ut, qt, spread, enter, weight = operands
        return call(
            functools.partial(project_first_body, sub),
            (jax.ShapeDtypeStruct((count * W, channels), BF16), jax.ShapeDtypeStruct((count * W, block_width), BF16)),
            (steps,),
            [
                pl.BlockSpec((count * W, step_channels), lambda i, s: (first // count, i)),
                pl.BlockSpec((count * W, step_channels), lambda i, s: (first // count, i)),
                pl.BlockSpec((W, wide), lambda i, s: (0, i)),
                pl.BlockSpec((count, modes, step_channels), lambda i, s: (first // count, 0, i)),
                pl.BlockSpec((step_channels, block_width), lambda i, s: (i, jnp.where(s[4] == 0, chan_count - 1, 0))),
            ],
            (
                pl.BlockSpec((count * W, step_channels), lambda i, s: (0, i)),
                pl.BlockSpec((count * W, block_width), lambda i, s: (0, 0)),
            ),
            prefetch=1,
            scratch=[pltpu.VMEM((count * W, block_width), F32)],
            flops=2 * count * W * channels * (block_width + modes * CB // 8),
            nbytes=2 * channels * (block_width + 4 * count * W),
            vmem=60,
            name="project_first",
        )(info, ut, qt, spread, enter, weight)

    def project_rest(count, info, mixed, weight, widths):
        starts = [sum(widths[:k]) * per_out for k in range(len(widths) + 1)]
        number = sum(widths)
        return call(
            functools.partial(project_rest_body, starts),
            [jax.ShapeDtypeStruct((count * W, width * block_width), BF16) for width in widths],
            (number * per_out,),
            [
                pl.BlockSpec((count * W, channels), lambda i, s: (0, 0)),
                pl.BlockSpec((channels, tile), lambda i, s: (0, column(number - 1 - i // per_out, lax.rem(i, per_out), s))),
            ],
            [
                pl.BlockSpec(
                    (count * W, tile), lambda i, s, k=k: (0, jnp.clip(i - starts[k], 0, starts[k + 1] - starts[k] - 1))
                )
                for k in range(len(widths))
            ],
            prefetch=1,
            flops=2 * count * W * channels * number * block_width,
            nbytes=2 * channels * number * block_width,
            vmem=60,
            name="project_rest",
        )(info, mixed, weight)

    def finish(first, count, buffer, own, parts):
        fresh = buffer is None
        rows = count * W
        specs = [pl.BlockSpec((rows, block_width), lambda i, s, at=at: (0, at)) for _, at in [*own, *parts]]
        arrays = [array for array, _ in [*own, *parts]]
        if not fresh:
            specs = specs + [pl.BlockSpec(memory_space=pl.ANY)]
            arrays.append(buffer)
        return call(
            functools.partial(finish_body, len(own), fresh, rows),
            jax.ShapeDtypeStruct((block_width, slots), BF16),
            (1,),
            specs,
            pl.BlockSpec((block_width, slots if fresh else rows), lambda i, s: (0, 0 if fresh else first // count)),
            prefetch=1,
            aliases=None if fresh else {len(arrays): 0},
            nbytes=(len(parts) + 2) * rows * block_width * 2,
            name="finish",
        )(info, *arrays)

    def value(entry):
        array, at = entry
        return array if array.shape[1] == block_width else array[:, at * block_width : (at + 1) * block_width]

    def hop(step, array):
        return lax.ppermute(array, "chan", [(step - 1, step), (chan_count - step, chan_count - step - 1)])

    def tied(value, *after):
        return lax.optimization_barrier((value, *after))[0]

    def branch(count):
        pieces = [(first, min(lead, count - first)) for first in range(0, count, lead)]

        def run(operands):
            weight = operands[-1]
            held, buffer = info, None
            sums, got = [{} for _ in pieces], [{} for _ in pieces]

            def send(p, step, block, *after):
                mine = value(sums[p][block])
                if step > 1:
                    mine = (mine.astype(F32) + value(got[p][step - 1, block]).astype(F32)).astype(BF16)
                mine = tied(mine, *after) if after else mine
                lands = chan_count - 1 - block if step == half else block
                got[p][step, lands] = hop(step, mine), 0
                return mine

            def sent(step):
                return range(chan_count - 1, step - 1, -1) if step <= half else range(chan_count - step - 1, -1, -1)

            last = chan_count - 1
            for p, (first, size) in enumerate(pieces):
                mixed, far = project_first(first, size, held, operands)
                sums[p][last] = far, 0
                send(p, 1, last)
                held = tied(held, far)
                if p + 1 < len(pieces) and last > 2:
                    joined, near = project_rest(size, held, mixed, weight, [last - 1, 1])
                    came = hop(1, joined)
                    for block in range(1, last):
                        sums[p][block] = joined, last - 1 - block
                        got[p][1, block] = came, last - 1 - block
                else:
                    *apart, near = project_rest(size, held, mixed, weight, [1] * last)
                    for block in range(last - 1, 0, -1):
                        sums[p][block] = apart[last - 1 - block], 0
                        send(p, 1, block)
                sums[p][0] = near, 0
                held = tied(held, near)
                if p + 1 < len(pieces):
                    held = tied(held, send(p, 2, last))
            passed = info

            def final(p, step):
                return got[p][step, step if step < half else chan_count - 1 - step]

            for p, (first, size) in enumerate(pieces):
                for step in range(2, chan_count):
                    for block in sent(step):
                        lands = chan_count - 1 - block if step == half else block
                        if (step, lands) not in got[p]:
                            early = step > half and p + 1 < len(pieces)
                            passed = send(p, step, block, *((final(p, 1)[0], passed) if early else ()))
                own = [sums[p][k] for k in range(half)]
                mine = [final(p, step) for step in range(1, chan_count)]
                buffer = finish(first, size, buffer, own, mine)
            return buffer

        return run

    used = (length + (W - 1)) // W
    return lax.switch(used - 1, [branch(c + 1) for c in range(chunks)], (ut, qt, spread, enter, out_weight))


def solution(mesh):
    placed = (
        P(None, "chan", "ctx"),
        P(None, None, "chan"),
        P("ctx"),
        P("ctx"),
        P(None, "chan"),
        P(None, "chan"),
        P("chan"),
        P("chan", None),
    )
    body = functools.partial(shards, mesh.shape["chan"], mesh.shape["ctx"])
    return jax.shard_map(body, mesh=mesh, in_specs=placed, out_specs=P("chan", "ctx"), check_vma=False)
```
